256 devices in a mesh: fgrp: 8 (over z), tile: 16 (over y_lo, x, core), pol: 2 (over y_hi).
Axes of the slice: x: 4, y: 4 (y_hi: 2, y_lo: 2; y = y_hi * 2 + y_lo), z: 8, core: 2. Of those that a mesh axis runs over, the one named last changes fastest.
Arguments:
- voltages: bfloat16 [2, 2048, 131072], P(None, ('tile', 'pol'), 'fgrp'), may hold values from -4 to 4
- gains: float32 [2, 2048, 64], P(None, ('tile', 'pol')), may hold values from -4 to 4
Outputs:
- visibilities: float32 [64, 2, 2048, 2048], P('fgrp', None, ('tile', 'pol'))
The draws below stay inside these ranges and needn't reach their ends.
All inputs are finite; a program needn't handle non-finite values.
Results may differ from the reference program's by a relative error of at most 0.0039.
Values may be sent and summed in bfloat16 or wider, within the bound.
A program may use at most 128 MiB of HBM per device.

```python
import math
import jax
import jax.numpy as jnp
from jax import lax

INPUTS = 2048
NFFT = 4096
TAPS = 4
SPECTRA = 32
CHANNELS = 64
SAMPLES = 131072


def level_of(rng, shape, cuts, low, largest):
    def one(dim, shards_of):
        draws = jax.random.uniform(jax.random.fold_in(jax.random.fold_in(rng, 6), dim), (shards_of,), jnp.float32, low / len(cuts), largest / len(cuts))
        return jnp.repeat(jnp.exp(draws), shape[dim] // shards_of).reshape((-1,) + (1,) * (len(shape) - dim - 1))

    level = one(*cuts[0])
    for cut in cuts[1:]:
        level = level * one(*cut)
    return level


def normal_values(rng, extent, spread, reach, cuts=(), kind=jnp.bfloat16):
    array = spread * jax.random.normal(rng, extent, jnp.float32)
    if cuts:
        array = array * level_of(rng, extent, cuts, -0.22, 0.18)
    return jnp.clip(array, -reach, reach).astype(kind)


def setup_inputs(seed: int = 0) -> dict:
    key_of = jax.random.split(jax.random.key(seed), 3)
    voltages = normal_values(key_of[0], (2, INPUTS, SAMPLES), 1.0, 4.0, ((1, 32), (2, 8)))
    gains = normal_values(key_of[1], (2, INPUTS, CHANNELS), 1.0, 4.0, ((1, 32),), jnp.float32)
    return {"voltages": voltages, "gains": gains}


def make_taps(tap_count, length):
    span_total = tap_count * length
    position = jnp.arange(span_total, dtype=jnp.int32).astype(jnp.float32)
    centred = (position - span_total / 2 + 0.5) / length
    window = 0.5 - 0.5 * jnp.cos(2.0 * math.pi * (position + 0.5) / span_total)
    return (jnp.sinc(centred) * window).reshape(tap_count, length)

def dft_table(length, channels):
    sample = jnp.arange(length, dtype=jnp.int32)
    column = jnp.arange(channels, dtype=jnp.int32)
    phases = sample[:, None] * column[None, :] % length
    angles = phases.astype(jnp.float32) * (2.0 * math.pi / length)
    return jnp.concatenate([jnp.cos(angles), jnp.sin(angles)], axis=1) / math.sqrt(length)

def filter_sum(padded, filter_taps, spectra_count):
    result = filter_taps[0] * padded[:, :, 0:spectra_count, :].astype(jnp.float32)
    for tap_index in range(1, filter_taps.shape[0]):
        result = result + filter_taps[tap_index] * padded[:, :, tap_index:tap_index + spectra_count, :].astype(jnp.float32)
    return result

def transform(filtered, table, channels):
    inputs_count = filtered.shape[1]
    spectra_count = filtered.shape[2]
    rows_flat = filtered.reshape(2, inputs_count * spectra_count, filtered.shape[3])
    product = jnp.einsum('prk,kq->prq', rows_flat, table, precision=lax.Precision.HIGHEST, preferred_element_type=jnp.float32)
    real_part = product[0, :, :channels] + product[1, :, channels:]
    imag_part = product[1, :, :channels] - product[0, :, channels:]
    return (real_part.reshape(inputs_count, spectra_count, channels), imag_part.reshape(inputs_count, spectra_count, channels))

def apply_gain(real_part, imag_part, gain_block):
    gain_real = gain_block[0][:, None, :]
    gain_imag = gain_block[1][:, None, :]
    out_real = gain_real * real_part - gain_imag * imag_part
    out_imag = gain_real * imag_part + gain_imag * real_part
    return jnp.stack([out_real, out_imag]).astype(jnp.bfloat16)

def reference(voltages, gains):
    filter_taps = make_taps(TAPS, NFFT)
    table = dft_table(NFFT, CHANNELS)
    block_size = 64
    blocks_count = INPUTS // block_size
    voltage_blocks = jnp.moveaxis(voltages.reshape(2, blocks_count, block_size, SPECTRA, NFFT), 1, 0)
    gain_blocks = jnp.moveaxis(gains.reshape(2, blocks_count, block_size, CHANNELS), 1, 0)

    def channelize(pieces):
        frames, gain_block = pieces
        padded = jnp.concatenate([jnp.zeros((2, block_size, TAPS - 1, NFFT), jnp.bfloat16), frames], axis=2)
        filtered = filter_sum(padded, filter_taps, SPECTRA)
        real_part, imag_part = transform(filtered, table, CHANNELS)
        return apply_gain(real_part, imag_part, gain_block)
    spectra = lax.map(channelize, (voltage_blocks, gain_blocks))
    spectra = jnp.moveaxis(spectra, 0, 1).reshape(2, INPUTS, SPECTRA, CHANNELS)
    by_channel = jnp.transpose(spectra, (3, 0, 1, 2))
    norm_factor = SPECTRA ** (-0.5)

    def correlate(channel_data):
        left_real = channel_data[0]
        left_imag = channel_data[1]
        real_sum = jnp.dot(left_real, left_real.T, preferred_element_type=jnp.float32) + jnp.dot(left_imag, left_imag.T, preferred_element_type=jnp.float32)
        imag_sum = jnp.dot(left_imag, left_real.T, preferred_element_type=jnp.float32) - jnp.dot(left_real, left_imag.T, preferred_element_type=jnp.float32)
        return jnp.stack([real_sum, imag_sum]) * norm_factor
    return lax.map(correlate, by_channel)
```

```python
import functools
import math

import jax
import jax.numpy as jnp
import numpy as np
from jax import lax
from jax.experimental import pallas as pl
from jax.experimental.pallas import tpu as pltpu
from jax.sharding import PartitionSpec as P

NFFT = 4096
TAPS = 4
MESH = pl.DeviceIdType.MESH


def tap_table():
    total = TAPS * NFFT
    n = np.arange(total, dtype=np.float64)
    x = (n - total / 2 + 0.5) / NFFT
    window = 0.5 - 0.5 * np.cos(2.0 * np.pi * (n + 0.5) / total)
    taps = np.sinc(x) * window / math.sqrt(NFFT)
    return taps.reshape(TAPS, NFFT).astype(np.float32)


def rotation_table():
    k = np.arange(NFFT, dtype=np.int64)
    m = np.arange(8, dtype=np.int64)
    rows = []
    for step in (1, 8):
        angle = (k[None, :] * (step * m)[:, None] % NFFT) * (2.0 * np.pi / NFFT)
        rows += [np.cos(angle), np.sin(angle)]
    return np.stack(rows).astype(np.float32)


def swap_halves(v):
    return jnp.concatenate([v[:, 64:], v[:, :64]], axis=1)


def spectra_kernel(
    volt, gains, taps, rot, out,
    xbuf, gbuf, tbuf, rbuf, table, acc, sbuf, abuf, own,
    in_sem, a2a_send, a2a_recv, ag_send, ux_recv, vy_recv, pt_recv,
):
    z, tile, pol = lax.axis_index("fgrp"), lax.axis_index("tile"), lax.axis_index("pol")
    depth = 8
    core, x, y = tile % 2, (tile // 2) % 4, pol * 2 + tile // 8
    u, v = x + core * (y - x), y + core * (x - y)

    def plane(u2, v2):
        x2, y2 = u2 + core * (v2 - u2), v2 + core * (u2 - v2)
        return ((y2 % 2) * 4 + x2) * 2 + core, y2 // 2

    def device(u2, v2):
        t2, p2 = plane(u2, v2)
        return {"fgrp": z, "tile": t2, "pol": p2}

    def block(u2, v2):
        t2, p2 = plane(u2, v2)
        return t2 * 2 + p2

    up, um, vp, vm = (u + 1) % 4, (u + 3) % 4, (v + 1) % 4, (v + 3) % 4
    partner = {"fgrp": z, "tile": tile + 1 - 2 * core, "pol": pol}
    ring = [(z + dz) % depth for dz in range(depth)]

    barrier = pltpu.get_barrier_semaphore()
    plane_peers = [device(up, v), device(um, v), device(u, vp), device(u, vm), partner]
    for peer in plane_peers:
        pl.semaphore_signal(barrier, inc=1, device_id=peer, device_id_type=MESH)
    for dz in range(1, depth):
        pl.semaphore_signal(
            barrier, inc=1, device_id={"fgrp": ring[dz], "tile": tile, "pol": pol},
            device_id_type=MESH,
        )

    small = [
        pltpu.make_async_copy(rot, rbuf, in_sem.at[4]),
        pltpu.make_async_copy(taps, tbuf, in_sem.at[5]),
        pltpu.make_async_copy(gains, gbuf, in_sem.at[6]),
    ]
    frames = [
        pltpu.make_async_copy(volt.at[:, :, pl.ds(f * NFFT, NFFT)], xbuf.at[f], in_sem.at[f])
        for f in range(4)
    ]
    for copy in small + frames:
        copy.start()
    for copy in small:
        copy.wait()

    lanes = 256

    def make(i, carry):
        ks = pl.ds(pl.multiple_of(i * lanes, lanes), lanes)
        cb, sb = rbuf[0, :, ks], rbuf[1, :, ks]
        for a in range(0, 8, 2):
            cos, sin = [], []
            for step in (a, a + 1):
                ca, sa = rbuf[2, pl.ds(step, 1), ks], rbuf[3, pl.ds(step, 1), ks]
                cos.append(cb * ca - sb * sa)
                sin.append(sb * ca + cb * sa)
            for part, rows in ((0, cos), (64, sin)):
                value = jnp.concatenate(rows, axis=0)
                for t in range(TAPS):
                    tapped = value * tbuf[pl.ds(t, 1), ks]
                    hi = tapped.astype(jnp.bfloat16)
                    lo = (tapped - hi.astype(jnp.float32)).astype(jnp.bfloat16)
                    table[t, pl.ds(part + a * 8, 16), ks] = hi
                    table[t, pl.ds(128 + part + a * 8, 16), ks] = lo
        return carry

    lax.fori_loop(0, NFFT // lanes, make, 0)
    for copy in frames:
        copy.wait()

    def transform(t, carry):
        acc[t] = lax.dot_general(
            table[t], xbuf[...].reshape(512, NFFT), (((1,), (1,)), ((), ())),
            preferred_element_type=jnp.float32,
        )
        return carry

    lax.fori_loop(0, TAPS, transform, 0)

    lane = lax.broadcasted_iota(jnp.int32, (64, 128), 1)
    sign = jnp.where(lane < 64, 1.0, -1.0).astype(jnp.float32)
    g_re = jnp.transpose(jnp.concatenate([gbuf[0], gbuf[0]], axis=0))
    g_im = jnp.transpose(jnp.concatenate([gbuf[1], gbuf[1]], axis=0)) * -sign
    for j in range(7):
        total = None
        for f in range(4):
            t = f - j + 3
            if 0 <= t < TAPS:
                fs = pl.ds(f * 128, 128)
                term = acc[t, pl.ds(0, 128), fs] + acc[t, pl.ds(128, 128), fs]
                total = term if total is None else total + term
        raw = total[:64] + sign * swap_halves(total[64:])
        gained = g_re * raw + g_im * swap_halves(raw)
        for c in range(depth):
            sbuf[c, j] = gained[8 * c : 8 * c + 8]

    pl.semaphore_wait(barrier, depth + 4)
    turns = []
    for dz in (4, 3, 5, 2, 6, 1, 7):
        turn = pltpu.make_async_remote_copy(
            src_ref=sbuf.at[ring[dz]], dst_ref=abuf.at[z],
            send_sem=a2a_send.at[dz], recv_sem=a2a_recv.at[dz],
            device_id={"fgrp": ring[dz], "tile": tile, "pol": pol}, device_id_type=MESH,
        )
        turn.start()
        turns.append(turn)
    abuf[z] = sbuf[z]
    for turn in turns:
        turn.wait_recv()

    for d in range(depth):
        for j in range(4):
            value = abuf[d, j]
            if d > 0 and j < 3:
                value = value + abuf[d - 1, j + 4]
            own[:, 4 * d + j, :] = value
    mine = block(u, v)
    out[mine] = own[...].astype(jnp.bfloat16)

    started = []

    def send(b, half, recv_sem, to):
        ref = out.at[b] if half is None else out.at[b, pl.ds(4 * half, 4)]
        copy = pltpu.make_async_remote_copy(
            src_ref=ref, dst_ref=ref, send_sem=ag_send.at[len(started)], recv_sem=recv_sem,
            device_id=to, device_id_type=MESH,
        )
        copy.start()
        started.append(copy)

    def arrived(b, half, recv_sem):
        ref = out.at[b] if half is None else out.at[b, pl.ds(4 * half, 4)]
        pltpu.make_async_remote_copy(
            src_ref=ref, dst_ref=ref, send_sem=ag_send.at[0], recv_sem=recv_sem,
            device_id=partner, device_id_type=MESH,
        ).wait_recv()

    columns = [u, um, up, (u + 2) % 4]
    rows = [v, vm, vp, (v + 2) % 4]

    def spread(q, b):
        send(b, None, vy_recv.at[q, 0], device(u, vp))
        send(b, None, vy_recv.at[q, 1], device(u, vm))

    def share(q, r):
        send(block(columns[q], rows[r]), None, pt_recv.at[q, r], partner)

    def pass_on(q):
        b = block(columns[q], vm)
        arrived(b, None, vy_recv.at[q, 0])
        send(b, 0, vy_recv.at[q, 2], device(u, vp))
        share(q, 1)
        b = block(columns[q], vp)
        arrived(b, None, vy_recv.at[q, 1])
        send(b, 1, vy_recv.at[q, 3], device(u, vm))
        share(q, 2)

    def far(q):
        b = block(columns[q], rows[3])
        arrived(b, 0, vy_recv.at[q, 2])
        arrived(b, 1, vy_recv.at[q, 3])
        share(q, 3)

    send(mine, None, ux_recv.at[0], device(up, v))
    send(mine, None, ux_recv.at[1], device(um, v))
    spread(0, mine)
    share(0, 0)
    arrived(block(um, v), None, ux_recv.at[0])
    send(block(um, v), 0, ux_recv.at[2], device(up, v))
    spread(1, block(um, v))
    share(1, 0)
    arrived(block(up, v), None, ux_recv.at[1])
    send(block(up, v), 1, ux_recv.at[3], device(um, v))
    spread(2, block(up, v))
    share(2, 0)
    pass_on(0)
    opposite = block(columns[3], v)
    arrived(opposite, 0, ux_recv.at[2])
    arrived(opposite, 1, ux_recv.at[3])
    spread(3, opposite)
    share(3, 0)
    pass_on(1)
    pass_on(2)
    far(0)
    pass_on(3)
    far(1)
    far(2)
    far(3)
    for q in range(4):
        for r in range(4):
            arrived(mine, None, pt_recv.at[q, r])
    for turn in turns:
        turn.wait_send()
    for copy in started:
        copy.wait_send()


def correlate_kernel(norm, blocks, out):
    m = pl.program_id(0)
    mine = lax.axis_index("tile") * 2 + lax.axis_index("pol")
    count = blocks.shape[0]
    first = lax.broadcasted_iota(jnp.int32, (32, 128), 1) < 64
    a = blocks[mine, m]
    swapped = swap_halves(a)
    lhs = jnp.concatenate([a, jnp.where(first, swapped, -swapped)], axis=0)
    for q in range(0, count, 4):
        tiles = []
        for b in (q, q + 2):
            g, h = blocks[b, m], blocks[b + 1, m]
            re = jnp.where(first, g, swap_halves(h))
            im = jnp.where(first, swap_halves(g), h)
            tiles.append(jnp.concatenate([re, im], axis=0))
        rhs = jnp.concatenate(tiles, axis=1)
        vis = lax.dot_general(
            lhs, rhs, (((0,), (0,)), ((), ())), preferred_element_type=jnp.float32
        ) * norm
        out[0, 0, :, pl.ds(q * 64, 256)] = vis[:64]
        out[0, 1, :, pl.ds(q * 64, 256)] = vis[64:]


def body(voltages, gains):
    inputs, channels = voltages.shape[1], gains.shape[2]
    fgrp = lax.axis_size("fgrp")
    count = lax.axis_size("tile") * lax.axis_size("pol")
    spectra = voltages.shape[2] // NFFT * fgrp
    mine = channels // fgrp
    any_spec = pl.BlockSpec(memory_space=pl.ANY)
    vmem_spec = pl.BlockSpec(memory_space=pltpu.VMEM)
    dma = pltpu.SemaphoreType.DMA
    blocks = pl.pallas_call(
        spectra_kernel,
        out_shape=pltpu.VMEM((count, mine, spectra, 2 * inputs), jnp.bfloat16),
        in_specs=[any_spec] * 4,
        out_specs=vmem_spec,
        scratch_shapes=[
            pltpu.VMEM((4, 2, inputs, NFFT), jnp.bfloat16),
            pltpu.VMEM((2, inputs, channels), jnp.float32),
            pltpu.VMEM((TAPS, NFFT), jnp.float32),
            pltpu.VMEM((4, 8, NFFT), jnp.float32),
            pltpu.VMEM((TAPS, 4 * channels, NFFT), jnp.bfloat16),
            pltpu.VMEM((TAPS, 4 * channels, 8 * inputs), jnp.float32),
            pltpu.VMEM((fgrp, 7, mine, 2 * inputs), jnp.float32),
            pltpu.VMEM((fgrp, 7, mine, 2 * inputs), jnp.float32),
            pltpu.VMEM((mine, spectra, 2 * inputs), jnp.float32),
            dma((7,)), dma((fgrp,)), dma((fgrp,)), dma((40,)), dma((4,)), dma((4, 4)), dma((4, 4)),
        ],
        compiler_params=pltpu.CompilerParams(
            collective_id=0, has_side_effects=True, vmem_limit_bytes=32 * 1024 * 1024
        ),
        name="spectra",
    )(voltages, gains, jnp.asarray(tap_table()), jnp.asarray(rotation_table()))
    return pl.pallas_call(
        functools.partial(correlate_kernel, 1.0 / math.sqrt(spectra)),
        out_shape=jax.ShapeDtypeStruct((mine, 2, inputs, count * inputs), jnp.float32),
        grid=(mine,),
        in_specs=[vmem_spec],
        out_specs=pl.BlockSpec((1, 2, inputs, count * inputs), lambda m: (m, 0, 0, 0)),
        compiler_params=pltpu.CompilerParams(vmem_limit_bytes=16 * 1024 * 1024),
        name="correlate",
    )(blocks)


def solution(mesh):
    return jax.shard_map(
        body,
        mesh=mesh,
        in_specs=(P(None, ("tile", "pol"), "fgrp"), P(None, ("tile", "pol"), None)),
        out_specs=P("fgrp", None, ("tile", "pol"), None),
        check_vma=False,
    )
```

```python
import functools
import math

import jax
import jax.numpy as jnp
import numpy as np
from jax import lax
from jax.experimental import pallas as pl
from jax.experimental.pallas import tpu as pltpu
from jax.sharding import PartitionSpec as P

NFFT = 4096
TAPS = 4
MESH = pl.DeviceIdType.MESH


def tap_table():
    total = TAPS * NFFT
    n = np.arange(total, dtype=np.float64)
    x = (n - total / 2 + 0.5) / NFFT
    window = 0.5 - 0.5 * np.cos(2.0 * np.pi * (n + 0.5) / total)
    taps = np.sinc(x) * window / math.sqrt(NFFT)
    return taps.reshape(TAPS, NFFT).astype(np.float32)


def rotation_table():
    k = np.arange(NFFT, dtype=np.int64)
    m = np.arange(8, dtype=np.int64)
    rows = []
    for step in (1, 8):
        angle = (k[None, :] * (step * m)[:, None] % NFFT) * (2.0 * np.pi / NFFT)
        rows += [np.cos(angle), np.sin(angle)]
    return np.stack(rows).astype(np.float32)


def swap_halves(v):
    return jnp.concatenate([v[:, 64:], v[:, :64]], axis=1)


def spectra_kernel(
    volt, gains, taps, rot, out,
    xbuf, gbuf, tbuf, rbuf, table, acc, sbuf, abuf, own,
    in_sem, a2a_send, a2a_recv, ag_send, ux_recv, vy_recv, pt_recv,
):
    z, tile, pol = lax.axis_index("fgrp"), lax.axis_index("tile"), lax.axis_index("pol")
    depth = 8
    core, x, y = tile % 2, (tile // 2) % 4, pol * 2 + tile // 8
    u, v = x + core * (y - x), y + core * (x - y)

    def plane(u2, v2):
        x2, y2 = u2 + core * (v2 - u2), v2 + core * (u2 - v2)
        return ((y2 % 2) * 4 + x2) * 2 + core, y2 // 2

    def device(u2, v2):
        t2, p2 = plane(u2, v2)
        return {"fgrp": z, "tile": t2, "pol": p2}

    def block(u2, v2):
        t2, p2 = plane(u2, v2)
        return t2 * 2 + p2

    partner = {"fgrp": z, "tile": tile + 1 - 2 * core, "pol": pol}
    ring = [(z + dz) % depth for dz in range(depth)]

    barrier = pltpu.get_barrier_semaphore()
    plane_peers = [device((u + d) % 4, v) for d in (1, 2, 3)] + [device(u, (v + d) % 4) for d in (1, 2, 3)]
    plane_peers.append(partner)
    for peer in plane_peers:
        pl.semaphore_signal(barrier, inc=1, device_id=peer, device_id_type=MESH)
    for dz in range(1, depth):
        pl.semaphore_signal(
            barrier, inc=1, device_id={"fgrp": ring[dz], "tile": tile, "pol": pol},
            device_id_type=MESH,
        )

    small = [
        pltpu.make_async_copy(rot, rbuf, in_sem.at[4]),
        pltpu.make_async_copy(taps, tbuf, in_sem.at[5]),
        pltpu.make_async_copy(gains, gbuf, in_sem.at[6]),
    ]
    frames = [
        pltpu.make_async_copy(volt.at[:, :, pl.ds(f * NFFT, NFFT)], xbuf.at[f], in_sem.at[f])
        for f in range(4)
    ]
    for copy in small + frames:
        copy.start()
    for copy in small:
        copy.wait()

    lanes = 256

    def make(i, carry):
        ks = pl.ds(pl.multiple_of(i * lanes, lanes), lanes)
        cb, sb = rbuf[0, :, ks], rbuf[1, :, ks]
        for a in range(0, 8, 2):
            cos, sin = [], []
            for step in (a, a + 1):
                ca, sa = rbuf[2, pl.ds(step, 1), ks], rbuf[3, pl.ds(step, 1), ks]
                cos.append(cb * ca - sb * sa)
                sin.append(sb * ca + cb * sa)
            for part, rows in ((0, cos), (64, sin)):
                value = jnp.concatenate(rows, axis=0)
                high, low = pl.ds(part + a * 8, 16), pl.ds(128 + part + a * 8, 16)
                for t in (1, 2):
                    tapped = value * tbuf[pl.ds(t, 1), ks]
                    rounded = tapped.astype(jnp.bfloat16)
                    table[t - 1, high, ks] = rounded
                    table[t - 1, low, ks] = (tapped - rounded.astype(jnp.float32)).astype(jnp.bfloat16)
                table[2, high, ks] = (value * tbuf[pl.ds(0, 1), ks]).astype(jnp.bfloat16)
                table[2, low, ks] = (value * tbuf[pl.ds(3, 1), ks]).astype(jnp.bfloat16)
        return carry

    lax.fori_loop(0, NFFT // lanes, make, 0)
    for copy in frames:
        copy.wait()

    def transform(part, carry):
        acc[part] = lax.dot_general(
            table[part], xbuf[...].reshape(512, NFFT), (((1,), (1,)), ((), ())),
            preferred_element_type=jnp.float32,
        )
        return carry

    lax.fori_loop(0, 3, transform, 0)

    lane = lax.broadcasted_iota(jnp.int32, (64, 128), 1)
    sign = jnp.where(lane < 64, 1.0, -1.0).astype(jnp.float32)
    g_re = jnp.transpose(jnp.concatenate([gbuf[0], gbuf[0]], axis=0))
    g_im = jnp.transpose(jnp.concatenate([gbuf[1], gbuf[1]], axis=0)) * -sign
    for j in range(7):
        total = None
        for f in range(4):
            t = f - j + 3
            if 0 <= t < TAPS:
                fs = pl.ds(f * 128, 128)
                if t in (1, 2):
                    term = acc[t - 1, pl.ds(0, 128), fs] + acc[t - 1, pl.ds(128, 128), fs]
                else:
                    term = acc[2, pl.ds(128 if t else 0, 128), fs]
                total = term if total is None else total + term
        raw = total[:64] + sign * swap_halves(total[64:])
        gained = g_re * raw + g_im * swap_halves(raw)
        for c in range(depth):
            sbuf[c, j] = gained[8 * c : 8 * c + 8]

    pl.semaphore_wait(barrier, depth + 6)
    turns = []
    for dz in (4, 3, 5, 2, 6, 1, 7):
        turn = pltpu.make_async_remote_copy(
            src_ref=sbuf.at[ring[dz]], dst_ref=abuf.at[z],
            send_sem=a2a_send.at[dz], recv_sem=a2a_recv.at[dz],
            device_id={"fgrp": ring[dz], "tile": tile, "pol": pol}, device_id_type=MESH,
        )
        turn.start()
        turns.append(turn)
    abuf[z] = sbuf[z]
    for turn in turns:
        turn.wait_recv()

    for d in range(depth):
        for j in range(4):
            value = abuf[d, j]
            if d > 0 and j < 3:
                value = value + abuf[d - 1, j + 4]
            own[:, 4 * d + j, :] = value
    mine = block(u, v)
    out[mine] = own[...].astype(jnp.bfloat16)

    started = []
    columns, rows = [u, (u + 3) % 4, (u + 1) % 4, (u + 2) % 4], [v, (v + 3) % 4, (v + 1) % 4, (v + 2) % 4]

    def send(b, recv_sem, to):
        copy = pltpu.make_async_remote_copy(
            src_ref=out.at[b], dst_ref=out.at[b], send_sem=ag_send.at[len(started)],
            recv_sem=recv_sem, device_id=to, device_id_type=MESH,
        )
        copy.start()
        started.append(copy)

    def arrived(b, recv_sem):
        pltpu.make_async_remote_copy(
            src_ref=out.at[b], dst_ref=out.at[b], send_sem=ag_send.at[0],
            recv_sem=recv_sem, device_id=partner, device_id_type=MESH,
        ).wait_recv()

    def spread(q):
        b = block(columns[q], v)
        send(b, vy_recv.at[q, 3], device(u, rows[3]))
        send(b, vy_recv.at[q, 1], device(u, rows[2]))
        send(b, vy_recv.at[q, 2], device(u, rows[1]))
        send(b, pt_recv.at[q, 0], partner)

    send(mine, ux_recv.at[3], device(columns[3], v))
    send(mine, ux_recv.at[1], device(columns[2], v))
    send(mine, ux_recv.at[2], device(columns[1], v))
    spread(0)
    for q in (1, 2, 3):
        arrived(block(columns[q], v), ux_recv.at[q])
        spread(q)
    for q in range(4):
        for r in (1, 2, 3):
            b = block(columns[q], rows[r])
            arrived(b, vy_recv.at[q, r])
            send(b, pt_recv.at[q, r], partner)
    for q in range(4):
        for r in range(4):
            arrived(mine, pt_recv.at[q, r])
    for turn in turns:
        turn.wait_send()
    for copy in started:
        copy.wait_send()


def correlate_kernel(norm, blocks, out, vis, sems):
    mine = lax.axis_index("tile") * 2 + lax.axis_index("pol")
    count, channels = blocks.shape[0], blocks.shape[1]
    first = lax.broadcasted_iota(jnp.int32, (32, 128), 1) < 64

    def write(m, part):
        return pltpu.make_async_copy(vis.at[m, part], out.at[m, part], sems.at[m, part])

    def channel(m, carry):
        a = blocks[mine, m]
        swapped = swap_halves(a)
        lhs = jnp.concatenate([a, jnp.where(first, swapped, -swapped)], axis=0)
        for q in range(0, count, 4):
            tiles = []
            for b in (q, q + 2):
                g, h = blocks[b, m], blocks[b + 1, m]
                re = jnp.where(first, g, swap_halves(h))
                im = jnp.where(first, swap_halves(g), h)
                tiles.append(jnp.concatenate([re, im], axis=0))
            rhs = jnp.concatenate(tiles, axis=1)
            product = lax.dot_general(
                lhs, rhs, (((0,), (0,)), ((), ())), preferred_element_type=jnp.float32
            ) * norm
            vis[m, 0, :, pl.ds(q * 64, 256)] = product[:64]
            vis[m, 1, :, pl.ds(q * 64, 256)] = product[64:]
        write(m, 0).start()
        write(m, 1).start()
        return carry

    lax.fori_loop(0, channels, channel, 0)
    for m in range(channels):
        write(m, 0).wait()
        write(m, 1).wait()


def body(voltages, gains):
    inputs, channels = voltages.shape[1], gains.shape[2]
    fgrp = lax.axis_size("fgrp")
    count = lax.axis_size("tile") * lax.axis_size("pol")
    spectra = voltages.shape[2] // NFFT * fgrp
    mine = channels // fgrp
    any_spec = pl.BlockSpec(memory_space=pltpu.HBM)
    vmem_spec = pl.BlockSpec(memory_space=pltpu.VMEM)
    dma = pltpu.SemaphoreType.DMA
    blocks = pl.pallas_call(
        spectra_kernel,
        out_shape=pltpu.VMEM((count, mine, spectra, 2 * inputs), jnp.bfloat16),
        in_specs=[any_spec] * 4,
        out_specs=vmem_spec,
        scratch_shapes=[
            pltpu.VMEM((4, 2, inputs, NFFT), jnp.bfloat16),
            pltpu.VMEM((2, inputs, channels), jnp.float32),
            pltpu.VMEM((TAPS, NFFT), jnp.float32),
            pltpu.VMEM((4, 8, NFFT), jnp.float32),
            pltpu.VMEM((3, 4 * channels, NFFT), jnp.bfloat16),
            pltpu.VMEM((3, 4 * channels, 8 * inputs), jnp.float32),
            pltpu.VMEM((fgrp, 7, mine, 2 * inputs), jnp.float32),
            pltpu.VMEM((fgrp, 7, mine, 2 * inputs), jnp.float32),
            pltpu.VMEM((mine, spectra, 2 * inputs), jnp.float32),
            dma((7,)), dma((fgrp,)), dma((fgrp,)), dma((40,)), dma((4,)), dma((4, 4)), dma((4, 4)),
        ],
        compiler_params=pltpu.CompilerParams(
            collective_id=0, has_side_effects=True, vmem_limit_bytes=32 * 1024 * 1024
        ),
        name="spectra",
    )(*[
        pltpu.with_memory_space_constraint(operand, pltpu.HBM)
        for operand in (voltages, gains, jnp.asarray(tap_table()), jnp.asarray(rotation_table()))
    ])
    vis_shape = (mine, 2, inputs, count * inputs)
    return pl.pallas_call(
        functools.partial(correlate_kernel, 1.0 / math.sqrt(spectra)),
        out_shape=jax.ShapeDtypeStruct(vis_shape, jnp.float32),
        in_specs=[vmem_spec],
        out_specs=any_spec,
        scratch_shapes=[pltpu.VMEM(vis_shape, jnp.float32), dma((mine, 2))],
        compiler_params=pltpu.CompilerParams(vmem_limit_bytes=16 * 1024 * 1024),
        name="correlate",
    )(blocks)


def solution(mesh):
    return jax.shard_map(
        body,
        mesh=mesh,
        in_specs=(P(None, ("tile", "pol"), "fgrp"), P(None, ("tile", "pol"), None)),
        out_specs=P("fgrp", None, ("tile", "pol"), None),
        check_vma=False,
    )
```

```python
import functools
import math

import jax
import jax.numpy as jnp
import numpy as np
from jax import lax
from jax.experimental import pallas as pl
from jax.experimental.pallas import tpu as pltpu
from jax.sharding import PartitionSpec as P

NFFT = 4096
TAPS = 4
MESH = pl.DeviceIdType.MESH


def tap_table():
    total = TAPS * NFFT
    n = np.arange(total, dtype=np.float64)
    x = (n - total / 2 + 0.5) / NFFT
    window = 0.5 - 0.5 * np.cos(2.0 * np.pi * (n + 0.5) / total)
    taps = np.sinc(x) * window / math.sqrt(NFFT)
    return taps.reshape(TAPS, NFFT).astype(np.float32)


def rotation_table():
    k = np.arange(NFFT, dtype=np.int64)
    m = np.arange(8, dtype=np.int64)
    rows = []
    for step in (1, 8):
        angle = (k[None, :] * (step * m)[:, None] % NFFT) * (2.0 * np.pi / NFFT)
        rows += [np.cos(angle), np.sin(angle)]
    return np.stack(rows).astype(np.float32)


def swap_halves(v):
    return jnp.concatenate([v[:, 64:], v[:, :64]], axis=1)


def spectra_kernel(
    volt, gains, taps, rot, out,
    xbuf, gbuf, tbuf, rbuf, table, acc, wide_send, wide, thin_send, thin, own,
    in_sem, a2a_send, a2a_recv, ag_send, ux_recv, vy_recv, pt_recv,
):
    z, tile, pol = lax.axis_index("fgrp"), lax.axis_index("tile"), lax.axis_index("pol")
    depth = 8
    core, x, y = tile % 2, (tile // 2) % 4, pol * 2 + tile // 8
    u, v = x + core * (y - x), y + core * (x - y)

    def plane(u2, v2):
        x2, y2 = u2 + core * (v2 - u2), v2 + core * (u2 - v2)
        return ((y2 % 2) * 4 + x2) * 2 + core, y2 // 2

    def device(u2, v2):
        t2, p2 = plane(u2, v2)
        return {"fgrp": z, "tile": t2, "pol": p2}

    def block(u2, v2):
        t2, p2 = plane(u2, v2)
        return t2 * 2 + p2

    partner = {"fgrp": z, "tile": tile + 1 - 2 * core, "pol": pol}
    ring = [(z + dz) % depth for dz in range(depth)]

    barrier = pltpu.get_barrier_semaphore()
    plane_peers = [device((u + d) % 4, v) for d in (1, 2, 3)] + [device(u, (v + d) % 4) for d in (1, 2, 3)]
    plane_peers.append(partner)
    for peer in plane_peers:
        pl.semaphore_signal(barrier, inc=1, device_id=peer, device_id_type=MESH)
    for dz in range(1, depth):
        pl.semaphore_signal(
            barrier, inc=1, device_id={"fgrp": ring[dz], "tile": tile, "pol": pol},
            device_id_type=MESH,
        )

    small = [
        pltpu.make_async_copy(rot, rbuf, in_sem.at[4]),
        pltpu.make_async_copy(taps, tbuf, in_sem.at[5]),
        pltpu.make_async_copy(gains, gbuf, in_sem.at[6]),
    ]
    frames = [
        pltpu.make_async_copy(volt.at[:, :, pl.ds(f * NFFT, NFFT)], xbuf.at[f], in_sem.at[f])
        for f in range(4)
    ]
    for copy in small + frames:
        copy.start()
    for copy in small:
        copy.wait()

    lanes = 256

    def make(i, carry):
        ks = pl.ds(pl.multiple_of(i * lanes, lanes), lanes)
        cb, sb = rbuf[0, :, ks], rbuf[1, :, ks]
        for a in range(0, 8, 2):
            cos, sin = [], []
            for step in (a, a + 1):
                ca, sa = rbuf[2, pl.ds(step, 1), ks], rbuf[3, pl.ds(step, 1), ks]
                cos.append(cb * ca - sb * sa)
                sin.append(sb * ca + cb * sa)
            for first, rows in ((0, cos), (64, sin)):
                value = jnp.concatenate(rows, axis=0)
                row = first + a * 8
                for t in (1, 2):
                    tapped = value * tbuf[pl.ds(t, 1), ks]
                    rounded = tapped.astype(jnp.bfloat16)
                    low = tapped - rounded.astype(jnp.float32)
                    table[pl.ds((t - 1) * 256 + row, 16), ks] = rounded
                    table[pl.ds((t - 1) * 256 + 128 + row, 16), ks] = low.astype(jnp.bfloat16)
                for t, base in ((0, 512), (3, 640)):
                    tapped = value * tbuf[pl.ds(t, 1), ks]
                    table[pl.ds(base + row, 16), ks] = tapped.astype(jnp.bfloat16)
        return carry

    lax.fori_loop(0, NFFT // lanes, make, 0)
    for copy in frames:
        copy.wait()
    acc[...] = lax.dot_general(
        table[...], xbuf[...].reshape(acc.shape[1], NFFT), (((1,), (1,)), ((), ())),
        preferred_element_type=jnp.float32,
    )

    lane = lax.broadcasted_iota(jnp.int32, (64, 128), 1)
    sign = jnp.where(lane < 64, 1.0, -1.0).astype(jnp.float32)
    g_re = jnp.transpose(jnp.concatenate([gbuf[0], gbuf[0]], axis=0))
    g_im = jnp.transpose(jnp.concatenate([gbuf[1], gbuf[1]], axis=0)) * -sign
    thin_of, wide_of = {0: 0, 3: 1, 6: 2}, {1: 0, 2: 1, 4: 2, 5: 3}
    for j in range(7):
        total = None
        for f in range(4):
            t = f - j + 3
            if 0 <= t < TAPS:
                fs = pl.ds(f * 128, 128)
                base = (512, 0, 256, 640)[t]
                term = acc[pl.ds(base, 128), fs]
                if t in (1, 2):
                    term = term + acc[pl.ds(base + 128, 128), fs]
                total = term if total is None else total + term
        raw = total[:64] + sign * swap_halves(total[64:])
        gained = g_re * raw + g_im * swap_halves(raw)
        for c in range(depth):
            if j in thin_of:
                thin_send[c, thin_of[j]] = gained[8 * c : 8 * c + 8].astype(jnp.bfloat16)
            else:
                wide_send[c, wide_of[j]] = gained[8 * c : 8 * c + 8]

    pl.semaphore_wait(barrier, depth + 6)
    turns = []
    for dz in (4, 3, 5, 2, 6, 1, 7):
        for k, (mine, theirs) in enumerate(((wide_send, wide), (thin_send, thin))):
            turn = pltpu.make_async_remote_copy(
                src_ref=mine.at[ring[dz]], dst_ref=theirs.at[z],
                send_sem=a2a_send.at[k, dz], recv_sem=a2a_recv.at[k, dz],
                device_id={"fgrp": ring[dz], "tile": tile, "pol": pol}, device_id_type=MESH,
            )
            turn.start()
            turns.append(turn)
    wide[z] = wide_send[z]
    thin[z] = thin_send[z]
    for turn in turns:
        turn.wait_recv()

    def partial(d, j):
        if j in thin_of:
            return thin[d, thin_of[j]].astype(jnp.float32)
        return wide[d, wide_of[j]]

    for d in range(depth):
        for j in range(4):
            value = partial(d, j)
            if d > 0 and j < 3:
                value = value + partial(d - 1, j + 4)
            own[:, 4 * d + j, :] = value
    mine = block(u, v)
    out[mine] = own[...].astype(jnp.bfloat16)

    started = []
    columns, rows = [u, (u + 3) % 4, (u + 1) % 4, (u + 2) % 4], [v, (v + 3) % 4, (v + 1) % 4, (v + 2) % 4]

    def send(b, recv_sem, to):
        copy = pltpu.make_async_remote_copy(
            src_ref=out.at[b], dst_ref=out.at[b], send_sem=ag_send.at[len(started)],
            recv_sem=recv_sem, device_id=to, device_id_type=MESH,
        )
        copy.start()
        started.append(copy)

    def arrived(b, recv_sem):
        pltpu.make_async_remote_copy(
            src_ref=out.at[b], dst_ref=out.at[b], send_sem=ag_send.at[0],
            recv_sem=recv_sem, device_id=partner, device_id_type=MESH,
        ).wait_recv()

    def spread(q):
        b = block(columns[q], v)
        send(b, vy_recv.at[q, 1], device(u, rows[2]))
        send(b, vy_recv.at[q, 2], device(u, rows[1]))
        send(b, vy_recv.at[q, 3], device(u, rows[3]))
        send(b, pt_recv.at[q, 0], partner)

    send(mine, ux_recv.at[1], device(columns[2], v))
    send(mine, ux_recv.at[2], device(columns[1], v))
    send(mine, ux_recv.at[3], device(columns[3], v))
    spread(0)
    for q in (1, 2, 3):
        arrived(block(columns[q], v), ux_recv.at[q])
        spread(q)
    for q in range(4):
        for r in (1, 2, 3):
            b = block(columns[q], rows[r])
            arrived(b, vy_recv.at[q, r])
            send(b, pt_recv.at[q, r], partner)
    for q in range(4):
        for r in range(4):
            arrived(mine, pt_recv.at[q, r])
    for turn in turns:
        turn.wait_send()
    for copy in started:
        copy.wait_send()


def correlate_kernel(norm, blocks, out, vis, sems):
    mine = lax.axis_index("tile") * 2 + lax.axis_index("pol")
    count, channels = blocks.shape[0], blocks.shape[1]
    first = lax.broadcasted_iota(jnp.int32, (32, 128), 1) < 64

    def write(m, part):
        return pltpu.make_async_copy(vis.at[m, part], out.at[m, part], sems.at[m, part])

    def channel(m, carry):
        a = blocks[mine, m]
        swapped = swap_halves(a)
        lhs = jnp.concatenate([a, jnp.where(first, swapped, -swapped)], axis=0)
        for q in range(0, count, 4):
            tiles = []
            for b in (q, q + 2):
                g, h = blocks[b, m], blocks[b + 1, m]
                re = jnp.where(first, g, swap_halves(h))
                im = jnp.where(first, swap_halves(g), h)
                tiles.append(jnp.concatenate([re, im], axis=0))
            rhs = jnp.concatenate(tiles, axis=1)
            product = lax.dot_general(
                lhs, rhs, (((0,), (0,)), ((), ())), preferred_element_type=jnp.float32
            ) * norm
            vis[m, 0, :, pl.ds(q * 64, 256)] = product[:64]
            vis[m, 1, :, pl.ds(q * 64, 256)] = product[64:]
        write(m, 0).start()
        write(m, 1).start()
        return carry

    lax.fori_loop(0, channels, channel, 0, unroll=True)
    for m in range(channels):
        write(m, 0).wait()
        write(m, 1).wait()


def body(voltages, gains):
    inputs, channels = voltages.shape[1], gains.shape[2]
    fgrp = lax.axis_size("fgrp")
    count = lax.axis_size("tile") * lax.axis_size("pol")
    spectra = voltages.shape[2] // NFFT * fgrp
    mine = channels // fgrp
    any_spec = pl.BlockSpec(memory_space=pltpu.HBM)
    vmem_spec = pl.BlockSpec(memory_space=pltpu.VMEM)
    dma = pltpu.SemaphoreType.DMA
    blocks = pl.pallas_call(
        spectra_kernel,
        out_shape=pltpu.VMEM((count, mine, spectra, 2 * inputs), jnp.bfloat16),
        in_specs=[any_spec] * 4,
        out_specs=vmem_spec,
        scratch_shapes=[
            pltpu.VMEM((4, 2, inputs, NFFT), jnp.bfloat16),
            pltpu.VMEM((2, inputs, channels), jnp.float32),
            pltpu.VMEM((TAPS, NFFT), jnp.float32),
            pltpu.VMEM((4, 8, NFFT), jnp.float32),
            pltpu.VMEM((12 * channels, NFFT), jnp.bfloat16),
            pltpu.VMEM((12 * channels, 8 * inputs), jnp.float32),
            pltpu.VMEM((fgrp, 4, mine, 2 * inputs), jnp.float32),
            pltpu.VMEM((fgrp, 4, mine, 2 * inputs), jnp.float32),
            pltpu.VMEM((fgrp, 3, mine, 2 * inputs), jnp.bfloat16),
            pltpu.VMEM((fgrp, 3, mine, 2 * inputs), jnp.bfloat16),
            pltpu.VMEM((mine, spectra, 2 * inputs), jnp.float32),
            dma((7,)), dma((2, fgrp)), dma((2, fgrp)), dma((40,)), dma((4,)), dma((4, 4)), dma((4, 4)),
        ],
        compiler_params=pltpu.CompilerParams(
            collective_id=0, has_side_effects=True, vmem_limit_bytes=32 * 1024 * 1024
        ),
        name="spectra",
    )(*[
        pltpu.with_memory_space_constraint(operand, pltpu.HBM)
        for operand in (voltages, gains, jnp.asarray(tap_table()), jnp.asarray(rotation_table()))
    ])
    vis_shape = (mine, 2, inputs, count * inputs)
    return pl.pallas_call(
        functools.partial(correlate_kernel, 1.0 / math.sqrt(spectra)),
        out_shape=jax.ShapeDtypeStruct(vis_shape, jnp.float32),
        in_specs=[vmem_spec],
        out_specs=any_spec,
        scratch_shapes=[pltpu.VMEM(vis_shape, jnp.float32), dma((mine, 2))],
        compiler_params=pltpu.CompilerParams(vmem_limit_bytes=16 * 1024 * 1024),
        name="correlate",
    )(blocks)


def solution(mesh):
    return jax.shard_map(
        body,
        mesh=mesh,
        in_specs=(P(None, ("tile", "pol"), "fgrp"), P(None, ("tile", "pol"), None)),
        out_specs=P("fgrp", None, ("tile", "pol"), None),
        check_vma=False,
    )
```

```python
import functools
import math

import jax
import jax.numpy as jnp
import numpy as np
from jax import lax
from jax.experimental import pallas as pl
from jax.experimental.pallas import tpu as pltpu
from jax.sharding import PartitionSpec as P

NFFT = 4096
TAPS = 4
MESH = pl.DeviceIdType.MESH


def tap_table():
    total = TAPS * NFFT
    n = np.arange(total, dtype=np.float64)
    x = (n - total / 2 + 0.5) / NFFT
    window = 0.5 - 0.5 * np.cos(2.0 * np.pi * (n + 0.5) / total)
    taps = np.sinc(x) * window / math.sqrt(NFFT)
    return taps.reshape(TAPS, NFFT).astype(np.float32)


def rotation_table():
    k = np.arange(NFFT, dtype=np.int64)
    m = np.arange(8, dtype=np.int64)
    rows = []
    for step in (1, 8):
        angle = (k[None, :] * (step * m)[:, None] % NFFT) * (2.0 * np.pi / NFFT)
        rows += [np.cos(angle), np.sin(angle)]
    return np.stack(rows).astype(np.float32)


def swap_halves(v):
    return jnp.concatenate([v[:, 64:], v[:, :64]], axis=1)


def spectra_kernel(
    volt, gains, taps, rot, out,
    xbuf, gbuf, tbuf, rbuf, table, acc, wide_send, wide, thin_send, thin, own,
    in_sem, a2a_send, a2a_recv, ag_send, ux_recv, vy_recv, pt_recv,
):
    z, tile, pol = lax.axis_index("fgrp"), lax.axis_index("tile"), lax.axis_index("pol")
    depth = 8
    core, x, y = tile % 2, (tile // 2) % 4, pol * 2 + tile // 8
    u, v = x + core * (y - x), y + core * (x - y)

    def plane(u2, v2):
        x2, y2 = u2 + core * (v2 - u2), v2 + core * (u2 - v2)
        return ((y2 % 2) * 4 + x2) * 2 + core, y2 // 2

    def device(u2, v2):
        t2, p2 = plane(u2, v2)
        return {"fgrp": z, "tile": t2, "pol": p2}

    def block(u2, v2):
        t2, p2 = plane(u2, v2)
        return t2 * 2 + p2

    partner = {"fgrp": z, "tile": tile + 1 - 2 * core, "pol": pol}
    ring = [(z + dz) % depth for dz in range(depth)]

    barrier = pltpu.get_barrier_semaphore()
    plane_peers = [device((u + d) % 4, v) for d in (1, 2, 3)] + [device(u, (v + d) % 4) for d in (1, 2, 3)]
    plane_peers.append(partner)
    for peer in plane_peers:
        pl.semaphore_signal(barrier, inc=1, device_id=peer, device_id_type=MESH)
    for dz in range(1, depth):
        pl.semaphore_signal(
            barrier, inc=1, device_id={"fgrp": ring[dz], "tile": tile, "pol": pol},
            device_id_type=MESH,
        )

    small = [
        pltpu.make_async_copy(rot, rbuf, in_sem.at[4]),
        pltpu.make_async_copy(taps, tbuf, in_sem.at[5]),
        pltpu.make_async_copy(gains, gbuf, in_sem.at[6]),
    ]
    frames = [
        pltpu.make_async_copy(volt.at[:, :, pl.ds(f * NFFT, NFFT)], xbuf.at[f], in_sem.at[f])
        for f in range(4)
    ]
    for copy in small + frames:
        copy.start()
    for copy in small:
        copy.wait()

    lanes = 256

    def make(i, carry):
        ks = pl.ds(pl.multiple_of(i * lanes, lanes), lanes)
        cb, sb = rbuf[0, :, ks], rbuf[1, :, ks]
        for a in range(0, 8, 2):
            cos, sin = [], []
            for step in (a, a + 1):
                ca, sa = rbuf[2, pl.ds(step, 1), ks], rbuf[3, pl.ds(step, 1), ks]
                cos.append(cb * ca - sb * sa)
                sin.append(sb * ca + cb * sa)
            for first, rows in ((0, cos), (64, sin)):
                value = jnp.concatenate(rows, axis=0)
                row = first + a * 8
                for t in (1, 2):
                    tapped = value * tbuf[pl.ds(t, 1), ks]
                    rounded = tapped.astype(jnp.bfloat16)
                    low = tapped - rounded.astype(jnp.float32)
                    table[pl.ds((t - 1) * 256 + row, 16), ks] = rounded
                    table[pl.ds((t - 1) * 256 + 128 + row, 16), ks] = low.astype(jnp.bfloat16)
                for t, base in ((0, 512), (3, 640)):
                    tapped = value * tbuf[pl.ds(t, 1), ks]
                    table[pl.ds(base + row, 16), ks] = tapped.astype(jnp.bfloat16)
        return carry

    lax.fori_loop(0, NFFT // lanes, make, 0)
    for copy in frames:
        copy.wait()
    acc[...] = lax.dot_general(
        table[...], xbuf[...].reshape(acc.shape[1], NFFT), (((1,), (1,)), ((), ())),
        preferred_element_type=jnp.float32,
    )

    lane = lax.broadcasted_iota(jnp.int32, (64, 128), 1)
    sign = jnp.where(lane < 64, 1.0, -1.0).astype(jnp.float32)
    g_re = jnp.transpose(jnp.concatenate([gbuf[0], gbuf[0]], axis=0))
    g_im = jnp.transpose(jnp.concatenate([gbuf[1], gbuf[1]], axis=0)) * -sign
    thin_of, wide_of = {0: 0, 3: 1, 6: 2}, {1: 0, 2: 1, 4: 2, 5: 3}
    for j in range(7):
        total = None
        for f in range(4):
            t = f - j + 3
            if 0 <= t < TAPS:
                fs = pl.ds(f * 128, 128)
                base = (512, 0, 256, 640)[t]
                term = acc[pl.ds(base, 128), fs]
                if t in (1, 2):
                    term = term + acc[pl.ds(base + 128, 128), fs]
                total = term if total is None else total + term
        raw = total[:64] + sign * swap_halves(total[64:])
        gained = g_re * raw + g_im * swap_halves(raw)
        for c in range(depth):
            if j in thin_of:
                thin_send[c, thin_of[j]] = gained[8 * c : 8 * c + 8].astype(jnp.bfloat16)
            else:
                wide_send[c, wide_of[j]] = gained[8 * c : 8 * c + 8]

    pl.semaphore_wait(barrier, depth + 6)
    turns = []
    for n in range(depth - 1):
        target = n + jnp.where(z <= n, 1, 0)
        dz = (target - z + depth) % depth
        for k, (mine, theirs) in enumerate(((wide_send, wide), (thin_send, thin))):
            turn = pltpu.make_async_remote_copy(
                src_ref=mine.at[target], dst_ref=theirs.at[z],
                send_sem=a2a_send.at[k, dz], recv_sem=a2a_recv.at[k, dz],
                device_id={"fgrp": target, "tile": tile, "pol": pol}, device_id_type=MESH,
            )
            turn.start()
            turns.append(turn)
    wide[z] = wide_send[z]
    thin[z] = thin_send[z]
    for turn in turns:
        turn.wait_recv()

    def partial(d, j):
        if j in thin_of:
            return thin[d, thin_of[j]].astype(jnp.float32)
        return wide[d, wide_of[j]]

    for d in range(depth):
        for j in range(4):
            value = partial(d, j)
            if d > 0 and j < 3:
                value = value + partial(d - 1, j + 4)
            own[:, 4 * d + j, :] = value
    mine = block(u, v)
    out[mine] = own[...].astype(jnp.bfloat16)

    started = []
    columns, rows = [u, (u + 3) % 4, (u + 1) % 4, (u + 2) % 4], [v, (v + 3) % 4, (v + 1) % 4, (v + 2) % 4]

    def send(b, recv_sem, to):
        copy = pltpu.make_async_remote_copy(
            src_ref=out.at[b], dst_ref=out.at[b], send_sem=ag_send.at[len(started)],
            recv_sem=recv_sem, device_id=to, device_id_type=MESH,
        )
        copy.start()
        started.append(copy)

    def arrived(b, recv_sem):
        pltpu.make_async_remote_copy(
            src_ref=out.at[b], dst_ref=out.at[b], send_sem=ag_send.at[0],
            recv_sem=recv_sem, device_id=partner, device_id_type=MESH,
        ).wait_recv()

    def spread(q):
        b = block(columns[q], v)
        send(b, vy_recv.at[q, 3], device(u, rows[3]))
        send(b, vy_recv.at[q, 1], device(u, rows[2]))
        send(b, vy_recv.at[q, 2], device(u, rows[1]))
        if q:
            send(b, pt_recv.at[q, 0], partner)

    send(mine, ux_recv.at[1], device(columns[2], v))
    send(mine, ux_recv.at[2], device(columns[1], v))
    send(mine, ux_recv.at[3], device(columns[3], v))
    send(mine, pt_recv.at[0, 0], partner)
    arrived(mine, pt_recv.at[0, 0])
    spread(0)
    for q in (1, 2, 3):
        arrived(block(columns[q], v), ux_recv.at[q])
        spread(q)
    for q in range(4):
        for r in (1, 2, 3):
            b = block(columns[q], rows[r])
            arrived(b, vy_recv.at[q, r])
            send(b, pt_recv.at[q, r], partner)
    for q in range(4):
        for r in range(4):
            if q or r:
                arrived(mine, pt_recv.at[q, r])
    for turn in turns:
        turn.wait_send()
    for copy in started:
        copy.wait_send()


def correlate_kernel(norm, blocks, out, vis, sems):
    mine = lax.axis_index("tile") * 2 + lax.axis_index("pol")
    count, channels = blocks.shape[0], blocks.shape[1]
    first = lax.broadcasted_iota(jnp.int32, (32, 128), 1) < 64

    def write(m, part):
        return pltpu.make_async_copy(vis.at[m, part], out.at[m, part], sems.at[m, part])

    def channel(m, carry):
        a = blocks[mine, m]
        swapped = swap_halves(a)
        lhs = jnp.concatenate([a, jnp.where(first, swapped, -swapped)], axis=0)
        for q in range(0, count, 4):
            tiles = []
            for b in (q, q + 2):
                g, h = blocks[b, m], blocks[b + 1, m]
                re = jnp.where(first, g, swap_halves(h))
                im = jnp.where(first, swap_halves(g), h)
                tiles.append(jnp.concatenate([re, im], axis=0))
            rhs = jnp.concatenate(tiles, axis=1)
            product = lax.dot_general(
                lhs, rhs, (((0,), (0,)), ((), ())), preferred_element_type=jnp.float32
            ) * norm
            vis[m, 0, :, pl.ds(q * 64, 256)] = product[:64]
            vis[m, 1, :, pl.ds(q * 64, 256)] = product[64:]
        write(m, 0).start()
        write(m, 1).start()
        return carry

    lax.fori_loop(0, channels, channel, 0, unroll=True)
    for m in range(channels):
        write(m, 0).wait()
        write(m, 1).wait()


def body(voltages, gains):
    inputs, channels = voltages.shape[1], gains.shape[2]
    fgrp = lax.axis_size("fgrp")
    count = lax.axis_size("tile") * lax.axis_size("pol")
    spectra = voltages.shape[2] // NFFT * fgrp
    mine = channels // fgrp
    any_spec = pl.BlockSpec(memory_space=pltpu.HBM)
    vmem_spec = pl.BlockSpec(memory_space=pltpu.VMEM)
    dma = pltpu.SemaphoreType.DMA
    blocks = pl.pallas_call(
        spectra_kernel,
        out_shape=pltpu.VMEM((count, mine, spectra, 2 * inputs), jnp.bfloat16),
        in_specs=[any_spec] * 4,
        out_specs=vmem_spec,
        scratch_shapes=[
            pltpu.VMEM((4, 2, inputs, NFFT), jnp.bfloat16),
            pltpu.VMEM((2, inputs, channels), jnp.float32),
            pltpu.VMEM((TAPS, NFFT), jnp.float32),
            pltpu.VMEM((4, 8, NFFT), jnp.float32),
            pltpu.VMEM((12 * channels, NFFT), jnp.bfloat16),
            pltpu.VMEM((12 * channels, 8 * inputs), jnp.float32),
            pltpu.VMEM((fgrp, 4, mine, 2 * inputs), jnp.float32),
            pltpu.VMEM((fgrp, 4, mine, 2 * inputs), jnp.float32),
            pltpu.VMEM((fgrp, 3, mine, 2 * inputs), jnp.bfloat16),
            pltpu.VMEM((fgrp, 3, mine, 2 * inputs), jnp.bfloat16),
            pltpu.VMEM((mine, spectra, 2 * inputs), jnp.float32),
            dma((7,)), dma((2, fgrp)), dma((2, fgrp)), dma((40,)), dma((4,)), dma((4, 4)), dma((4, 4)),
        ],
        compiler_params=pltpu.CompilerParams(
            collective_id=0, has_side_effects=True, vmem_limit_bytes=32 * 1024 * 1024
        ),
        name="spectra",
    )(*[
        pltpu.with_memory_space_constraint(operand, pltpu.HBM)
        for operand in (voltages, gains, jnp.asarray(tap_table()), jnp.asarray(rotation_table()))
    ])
    vis_shape = (mine, 2, inputs, count * inputs)
    return pl.pallas_call(
        functools.partial(correlate_kernel, 1.0 / math.sqrt(spectra)),
        out_shape=jax.ShapeDtypeStruct(vis_shape, jnp.float32),
        in_specs=[vmem_spec],
        out_specs=any_spec,
        scratch_shapes=[pltpu.VMEM(vis_shape, jnp.float32), dma((mine, 2))],
        compiler_params=pltpu.CompilerParams(vmem_limit_bytes=16 * 1024 * 1024),
        name="correlate",
    )(blocks)


def solution(mesh):
    return jax.shard_map(
        body,
        mesh=mesh,
        in_specs=(P(None, ("tile", "pol"), "fgrp"), P(None, ("tile", "pol"), None)),
        out_specs=P("fgrp", None, ("tile", "pol"), None),
        check_vma=False,
    )
```

```python
import functools
import math

import jax
import jax.numpy as jnp
import numpy as np
from jax import lax
from jax.experimental import pallas as pl
from jax.experimental.pallas import tpu as pltpu
from jax.sharding import PartitionSpec as P

NFFT = 4096
TAPS = 4
MESH = pl.DeviceIdType.MESH


def tap_table():
    total = TAPS * NFFT
    n = np.arange(total, dtype=np.float64)
    x = (n - total / 2 + 0.5) / NFFT
    window = 0.5 - 0.5 * np.cos(2.0 * np.pi * (n + 0.5) / total)
    taps = np.sinc(x) * window / math.sqrt(NFFT)
    return taps.reshape(TAPS, NFFT).astype(np.float32)


def rotation_table():
    k = np.arange(NFFT, dtype=np.int64)
    m = np.arange(8, dtype=np.int64)
    rows = []
    for step in (1, 8):
        angle = (k[None, :] * (step * m)[:, None] % NFFT) * (2.0 * np.pi / NFFT)
        rows += [np.cos(angle), np.sin(angle)]
    return np.stack(rows).astype(np.float32)


def swap_halves(v):
    return jnp.concatenate([v[:, 64:], v[:, :64]], axis=1)


def spectra_kernel(
    volt, gains, taps, rot, out,
    xbuf, gbuf, tbuf, rbuf, table, acc, wide_send, wide, thin_send, thin, own,
    in_sem, a2a_send, a2a_recv, ag_send, ux_recv, vy_recv, pt_recv,
):
    z, tile, pol = lax.axis_index("fgrp"), lax.axis_index("tile"), lax.axis_index("pol")
    depth = 8
    core, x, y = tile % 2, (tile // 2) % 4, pol * 2 + tile // 8
    u, v = x + core * (y - x), y + core * (x - y)

    def plane(u2, v2):
        x2, y2 = u2 + core * (v2 - u2), v2 + core * (u2 - v2)
        return ((y2 % 2) * 4 + x2) * 2 + core, y2 // 2

    def device(u2, v2):
        t2, p2 = plane(u2, v2)
        return {"fgrp": z, "tile": t2, "pol": p2}

    def block(u2, v2):
        t2, p2 = plane(u2, v2)
        return t2 * 2 + p2

    partner = {"fgrp": z, "tile": tile + 1 - 2 * core, "pol": pol}
    ring = [(z + dz) % depth for dz in range(depth)]

    barrier = pltpu.get_barrier_semaphore()
    plane_peers = [device((u + d) % 4, v) for d in (1, 2, 3)] + [device(u, (v + d) % 4) for d in (1, 2, 3)]
    plane_peers.append(partner)
    for peer in plane_peers:
        pl.semaphore_signal(barrier, inc=1, device_id=peer, device_id_type=MESH)
    for dz in range(1, depth):
        pl.semaphore_signal(
            barrier, inc=1, device_id={"fgrp": ring[dz], "tile": tile, "pol": pol},
            device_id_type=MESH,
        )

    small = [
        pltpu.make_async_copy(rot, rbuf, in_sem.at[4]),
        pltpu.make_async_copy(taps, tbuf, in_sem.at[5]),
        pltpu.make_async_copy(gains, gbuf, in_sem.at[6]),
    ]
    frames = [
        pltpu.make_async_copy(volt.at[:, :, pl.ds(f * NFFT, NFFT)], xbuf.at[f], in_sem.at[f])
        for f in range(4)
    ]
    for copy in small + frames:
        copy.start()
    for copy in small:
        copy.wait()

    lanes = 256

    def make(i, carry):
        ks = pl.ds(pl.multiple_of(i * lanes, lanes), lanes)
        cb, sb = rbuf[0, :, ks], rbuf[1, :, ks]
        for a in range(0, 8, 2):
            cos, sin = [], []
            for step in (a, a + 1):
                ca, sa = rbuf[2, pl.ds(step, 1), ks], rbuf[3, pl.ds(step, 1), ks]
                cos.append(cb * ca - sb * sa)
                sin.append(sb * ca + cb * sa)
            for first, rows in ((0, cos), (64, sin)):
                value = jnp.concatenate(rows, axis=0)
                row = first + a * 8
                for t in (1, 2):
                    tapped = value * tbuf[pl.ds(t, 1), ks]
                    rounded = tapped.astype(jnp.bfloat16)
                    low = tapped - rounded.astype(jnp.float32)
                    table[pl.ds((t - 1) * 256 + row, 16), ks] = rounded
                    table[pl.ds((t - 1) * 256 + 128 + row, 16), ks] = low.astype(jnp.bfloat16)
                for t, base in ((0, 512), (3, 640)):
                    tapped = value * tbuf[pl.ds(t, 1), ks]
                    table[pl.ds(base + row, 16), ks] = tapped.astype(jnp.bfloat16)
        return carry

    lax.fori_loop(0, NFFT // lanes, make, 0)
    for copy in frames:
        copy.wait()
    acc[...] = lax.dot_general(
        table[...], xbuf[...].reshape(acc.shape[1], NFFT), (((1,), (1,)), ((), ())),
        preferred_element_type=jnp.float32,
    )

    lane = lax.broadcasted_iota(jnp.int32, (64, 128), 1)
    sign = jnp.where(lane < 64, 1.0, -1.0).astype(jnp.float32)
    g_re = jnp.transpose(jnp.concatenate([gbuf[0], gbuf[0]], axis=0))
    g_im = jnp.transpose(jnp.concatenate([gbuf[1], gbuf[1]], axis=0)) * -sign
    thin_of, wide_of = {0: 0, 3: 1, 6: 2}, {1: 0, 2: 1, 4: 2, 5: 3}
    for j in range(7):
        total = None
        for f in range(4):
            t = f - j + 3
            if 0 <= t < TAPS:
                fs = pl.ds(f * 128, 128)
                base = (512, 0, 256, 640)[t]
                term = acc[pl.ds(base, 128), fs]
                if t in (1, 2):
                    term = term + acc[pl.ds(base + 128, 128), fs]
                total = term if total is None else total + term
        raw = total[:64] + sign * swap_halves(total[64:])
        gained = g_re * raw + g_im * swap_halves(raw)
        for c in range(depth):
            if j in thin_of:
                thin_send[c, thin_of[j]] = gained[8 * c : 8 * c + 8].astype(jnp.bfloat16)
            else:
                wide_send[c, wide_of[j]] = gained[8 * c : 8 * c + 8]

    pl.semaphore_wait(barrier, depth + 6)
    turns = []
    for n in range(depth - 1):
        target = n + jnp.where(z <= n, 1, 0)
        dz = (target - z + depth) % depth
        for k, (ours, theirs) in enumerate(((wide_send, wide), (thin_send, thin))):
            turn = pltpu.make_async_remote_copy(
                src_ref=ours.at[target], dst_ref=theirs.at[z],
                send_sem=a2a_send.at[k, dz], recv_sem=a2a_recv.at[k, dz],
                device_id={"fgrp": target, "tile": tile, "pol": pol}, device_id_type=MESH,
            )
            turn.start()
            turns.append(turn)
    wide[z] = wide_send[z]
    thin[z] = thin_send[z]
    def partial(d, j):
        if j in thin_of:
            return thin[d, thin_of[j]].astype(jnp.float32)
        return wide[d, wide_of[j]]

    mine = block(u, v)
    half = depth // 2

    def landed(source):
        for k, ref in enumerate((wide, thin)):
            pltpu.make_async_remote_copy(
                src_ref=ref.at[source], dst_ref=ref.at[source], send_sem=a2a_send.at[k, 0],
                recv_sem=a2a_recv.at[k, (z - source + depth) % depth],
                device_id=partner, device_id_type=MESH,
            ).wait_recv()

    def finish(h):
        for source in range(h * half, (h + 1) * half):
            pl.when(z != source)(functools.partial(landed, source))
        for n in range(half):
            d = h * half + n
            for j in range(4):
                value = partial(d, j)
                if d > 0 and j < 3:
                    value = value + partial(d - 1, j + 4)
                own[h, :, 4 * n + j, :] = value
        out[mine, h] = own[h].astype(jnp.bfloat16)

    started = []
    columns, rows = [u, (u + 3) % 4, (u + 1) % 4, (u + 2) % 4], [v, (v + 3) % 4, (v + 1) % 4, (v + 2) % 4]

    def send(b, h, recv_sem, to):
        copy = pltpu.make_async_remote_copy(
            src_ref=out.at[b, h], dst_ref=out.at[b, h], send_sem=ag_send.at[len(started)],
            recv_sem=recv_sem, device_id=to, device_id_type=MESH,
        )
        copy.start()
        started.append(copy)

    def arrived(b, h, recv_sem):
        pltpu.make_async_remote_copy(
            src_ref=out.at[b, h], dst_ref=out.at[b, h], send_sem=ag_send.at[0],
            recv_sem=recv_sem, device_id=partner, device_id_type=MESH,
        ).wait_recv()

    def along_u(h):
        send(mine, h, ux_recv.at[h, 1], device(columns[2], v))
        send(mine, h, ux_recv.at[h, 2], device(columns[1], v))
        send(mine, h, ux_recv.at[h, 3], device(columns[3], v))
        send(mine, h, pt_recv.at[h, 0, 0], partner)

    def along_v(h, q):
        b = block(columns[q], v)
        send(b, h, vy_recv.at[h, q, 3], device(u, rows[3]))
        send(b, h, vy_recv.at[h, q, 1], device(u, rows[2]))
        send(b, h, vy_recv.at[h, q, 2], device(u, rows[1]))

    def column(h, q):
        b = block(columns[q], v)
        arrived(b, h, ux_recv.at[h, q])
        along_v(h, q)
        send(b, h, pt_recv.at[h, q, 0], partner)

    def share(h, q):
        for r in (1, 2, 3):
            b = block(columns[q], rows[r])
            arrived(b, h, vy_recv.at[h, q, r])
            send(b, h, pt_recv.at[h, q, r], partner)

    finish(0)
    along_u(0)
    along_v(0, 0)
    finish(1)
    along_u(1)
    for q in (1, 2, 3):
        column(0, q)
    along_v(1, 0)
    share(0, 0)
    for q in (1, 2, 3):
        column(1, q)
    for q in (1, 2, 3):
        share(0, q)
    for q in range(4):
        share(1, q)
    for h in range(2):
        for q in range(4):
            for r in range(4):
                arrived(mine, h, pt_recv.at[h, q, r])
    for turn in turns:
        turn.wait_send()
    for copy in started:
        copy.wait_send()


def correlate_kernel(norm, blocks, out, vis, sems):
    mine = lax.axis_index("tile") * 2 + lax.axis_index("pol")
    count, channels = blocks.shape[0], blocks.shape[2]
    first = lax.broadcasted_iota(jnp.int32, (32, 128), 1) < 64

    def write(m, part):
        return pltpu.make_async_copy(vis.at[m, part], out.at[m, part], sems.at[m, part])

    def spectra(b, m):
        return jnp.concatenate([blocks[b, 0, m], blocks[b, 1, m]], axis=0)

    def channel(m, carry):
        a = spectra(mine, m)
        swapped = swap_halves(a)
        lhs = jnp.concatenate([a, jnp.where(first, swapped, -swapped)], axis=0)
        for q in range(0, count, 4):
            tiles = []
            for b in (q, q + 2):
                g, h = spectra(b, m), spectra(b + 1, m)
                re = jnp.where(first, g, swap_halves(h))
                im = jnp.where(first, swap_halves(g), h)
                tiles.append(jnp.concatenate([re, im], axis=0))
            rhs = jnp.concatenate(tiles, axis=1)
            product = lax.dot_general(
                lhs, rhs, (((0,), (0,)), ((), ())), preferred_element_type=jnp.float32
            ) * norm
            vis[m, 0, :, pl.ds(q * 64, 256)] = product[:64]
            vis[m, 1, :, pl.ds(q * 64, 256)] = product[64:]
        write(m, 0).start()
        write(m, 1).start()
        return carry

    lax.fori_loop(0, channels, channel, 0, unroll=True)
    for m in range(channels):
        write(m, 0).wait()
        write(m, 1).wait()


def body(voltages, gains):
    inputs, channels = voltages.shape[1], gains.shape[2]
    fgrp = lax.axis_size("fgrp")
    count = lax.axis_size("tile") * lax.axis_size("pol")
    spectra = voltages.shape[2] // NFFT * fgrp
    mine = channels // fgrp
    any_spec = pl.BlockSpec(memory_space=pltpu.HBM)
    vmem_spec = pl.BlockSpec(memory_space=pltpu.VMEM)
    dma = pltpu.SemaphoreType.DMA
    blocks = pl.pallas_call(
        spectra_kernel,
        out_shape=pltpu.VMEM((count, 2, mine, spectra // 2, 2 * inputs), jnp.bfloat16),
        in_specs=[any_spec] * 4,
        out_specs=vmem_spec,
        scratch_shapes=[
            pltpu.VMEM((4, 2, inputs, NFFT), jnp.bfloat16),
            pltpu.VMEM((2, inputs, channels), jnp.float32),
            pltpu.VMEM((TAPS, NFFT), jnp.float32),
            pltpu.VMEM((4, 8, NFFT), jnp.float32),
            pltpu.VMEM((12 * channels, NFFT), jnp.bfloat16),
            pltpu.VMEM((12 * channels, 8 * inputs), jnp.float32),
            pltpu.VMEM((fgrp, 4, mine, 2 * inputs), jnp.float32),
            pltpu.VMEM((fgrp, 4, mine, 2 * inputs), jnp.float32),
            pltpu.VMEM((fgrp, 3, mine, 2 * inputs), jnp.bfloat16),
            pltpu.VMEM((fgrp, 3, mine, 2 * inputs), jnp.bfloat16),
            pltpu.VMEM((2, mine, spectra // 2, 2 * inputs), jnp.float32),
            dma((7,)), dma((2, fgrp)), dma((2, fgrp)), dma((64,)), dma((2, 4)), dma((2, 4, 4)), dma((2, 4, 4)),
        ],
        compiler_params=pltpu.CompilerParams(
            collective_id=0, has_side_effects=True, vmem_limit_bytes=32 * 1024 * 1024
        ),
        name="spectra",
    )(*[
        pltpu.with_memory_space_constraint(operand, pltpu.HBM)
        for operand in (voltages, gains, jnp.asarray(tap_table()), jnp.asarray(rotation_table()))
    ])
    vis_shape = (mine, 2, inputs, count * inputs)
    return pl.pallas_call(
        functools.partial(correlate_kernel, 1.0 / math.sqrt(spectra)),
        out_shape=jax.ShapeDtypeStruct(vis_shape, jnp.float32),
        in_specs=[vmem_spec],
        out_specs=any_spec,
        scratch_shapes=[pltpu.VMEM(vis_shape, jnp.float32), dma((mine, 2))],
        compiler_params=pltpu.CompilerParams(vmem_limit_bytes=16 * 1024 * 1024),
        name="correlate",
    )(blocks)


def solution(mesh):
    return jax.shard_map(
        body,
        mesh=mesh,
        in_specs=(P(None, ("tile", "pol"), "fgrp"), P(None, ("tile", "pol"), None)),
        out_specs=P("fgrp", None, ("tile", "pol"), None),
        check_vma=False,
    )
```

```python
import functools
import math

import jax
import jax.numpy as jnp
import numpy as np
from jax import lax
from jax.experimental import pallas as pl
from jax.experimental.pallas import tpu as pltpu
from jax.sharding import PartitionSpec as P

NFFT = 4096
TAPS = 4
MESH = pl.DeviceIdType.MESH


def tap_table():
    total = TAPS * NFFT
    n = np.arange(total, dtype=np.float64)
    x = (n - total / 2 + 0.5) / NFFT
    window = 0.5 - 0.5 * np.cos(2.0 * np.pi * (n + 0.5) / total)
    taps = np.sinc(x) * window / math.sqrt(NFFT)
    return taps.reshape(TAPS, NFFT).astype(np.float32)


def rotation_table():
    k = np.arange(NFFT, dtype=np.int64)
    m = np.arange(8, dtype=np.int64)
    rows = []
    for step in (1, 8):
        angle = (k[None, :] * (step * m)[:, None] % NFFT) * (2.0 * np.pi / NFFT)
        rows += [np.cos(angle), np.sin(angle)]
    return np.stack(rows).astype(np.float32)


def swap_halves(v):
    return jnp.concatenate([v[:, 64:], v[:, :64]], axis=1)


def spectra_kernel(
    volt, gains, taps, rot, out,
    xbuf, gbuf, tbuf, rbuf, table, acc, wide_send, wide, thin_send, thin, own,
    in_sem, a2a_send, a2a_recv, ag_send, ux_recv, vy_recv, pt_recv,
):
    z, tile, pol = lax.axis_index("fgrp"), lax.axis_index("tile"), lax.axis_index("pol")
    depth = 8
    core, x, y = tile % 2, (tile // 2) % 4, pol * 2 + tile // 8
    u, v = x + core * (y - x), y + core * (x - y)

    def plane(u2, v2):
        x2, y2 = u2 + core * (v2 - u2), v2 + core * (u2 - v2)
        return ((y2 % 2) * 4 + x2) * 2 + core, y2 // 2

    def device(u2, v2):
        t2, p2 = plane(u2, v2)
        return {"fgrp": z, "tile": t2, "pol": p2}

    def block(u2, v2):
        t2, p2 = plane(u2, v2)
        return t2 * 2 + p2

    partner = {"fgrp": z, "tile": tile + 1 - 2 * core, "pol": pol}
    ring = [(z + dz) % depth for dz in range(depth)]

    barrier = pltpu.get_barrier_semaphore()
    plane_peers = [device((u + d) % 4, v) for d in (1, 2, 3)] + [device(u, (v + d) % 4) for d in (1, 2, 3)]
    plane_peers += [device((u + 2) % 4, (v + d) % 4) for d in (1, 2, 3)]
    plane_peers += [device((u + d) % 4, (v + 2) % 4) for d in (1, 3)]
    plane_peers.append(partner)
    for peer in plane_peers:
        pl.semaphore_signal(barrier, inc=1, device_id=peer, device_id_type=MESH)
    for dz in range(1, depth):
        pl.semaphore_signal(
            barrier, inc=1, device_id={"fgrp": ring[dz], "tile": tile, "pol": pol},
            device_id_type=MESH,
        )

    small = [
        pltpu.make_async_copy(rot, rbuf, in_sem.at[4]),
        pltpu.make_async_copy(taps, tbuf, in_sem.at[5]),
        pltpu.make_async_copy(gains, gbuf, in_sem.at[6]),
    ]
    frames = [
        pltpu.make_async_copy(volt.at[:, :, pl.ds(f * NFFT, NFFT)], xbuf.at[f], in_sem.at[f])
        for f in range(4)
    ]
    for copy in small + frames:
        copy.start()
    for copy in small:
        copy.wait()

    lanes = 256

    def make(i, carry):
        ks = pl.ds(pl.multiple_of(i * lanes, lanes), lanes)
        cb, sb = rbuf[0, :, ks], rbuf[1, :, ks]
        for a in range(0, 8, 2):
            cos, sin = [], []
            for step in (a, a + 1):
                ca, sa = rbuf[2, pl.ds(step, 1), ks], rbuf[3, pl.ds(step, 1), ks]
                cos.append(cb * ca - sb * sa)
                sin.append(sb * ca + cb * sa)
            for first, rows in ((0, cos), (64, sin)):
                value = jnp.concatenate(rows, axis=0)
                row = first + a * 8
                for t in (1, 2):
                    tapped = value * tbuf[pl.ds(t, 1), ks]
                    rounded = tapped.astype(jnp.bfloat16)
                    low = tapped - rounded.astype(jnp.float32)
                    table[pl.ds((t - 1) * 256 + row, 16), ks] = rounded
                    table[pl.ds((t - 1) * 256 + 128 + row, 16), ks] = low.astype(jnp.bfloat16)
                for t, base in ((0, 512), (3, 640)):
                    tapped = value * tbuf[pl.ds(t, 1), ks]
                    table[pl.ds(base + row, 16), ks] = tapped.astype(jnp.bfloat16)
        return carry

    lax.fori_loop(0, NFFT // lanes, make, 0)
    lane = lax.broadcasted_iota(jnp.int32, (64, 128), 1)
    sign = jnp.where(lane < 64, 1.0, -1.0).astype(jnp.float32)
    g_re = jnp.transpose(jnp.concatenate([gbuf[0], gbuf[0]], axis=0))
    g_im = jnp.transpose(jnp.concatenate([gbuf[1], gbuf[1]], axis=0)) * -sign
    for copy in frames:
        copy.wait()
    acc[...] = lax.dot_general(
        table[...], xbuf[...].reshape(acc.shape[1], NFFT), (((1,), (1,)), ((), ())),
        preferred_element_type=jnp.float32,
    )

    thin_of, wide_of = {0: 0, 3: 1, 6: 2}, {1: 0, 2: 1, 4: 2, 5: 3}
    for j in range(7):
        total = None
        for f in range(4):
            t = f - j + 3
            if 0 <= t < TAPS:
                fs = pl.ds(f * 128, 128)
                base = (512, 0, 256, 640)[t]
                term = acc[pl.ds(base, 128), fs]
                if t in (1, 2):
                    term = term + acc[pl.ds(base + 128, 128), fs]
                total = term if total is None else total + term
        raw = total[:64] + sign * swap_halves(total[64:])
        gained = g_re * raw + g_im * swap_halves(raw)
        for c in range(depth):
            if j in thin_of:
                thin_send[c, thin_of[j]] = gained[8 * c : 8 * c + 8].astype(jnp.bfloat16)
            else:
                wide_send[c, wide_of[j]] = gained[8 * c : 8 * c + 8]

    pl.semaphore_wait(barrier, depth + 11)
    turns = []
    for n in range(depth - 1):
        target = n + jnp.where(z <= n, 1, 0)
        dz = (target - z + depth) % depth
        for k, (ours, theirs) in enumerate(((wide_send, wide), (thin_send, thin))):
            turn = pltpu.make_async_remote_copy(
                src_ref=ours.at[target], dst_ref=theirs.at[z],
                send_sem=a2a_send.at[k, dz], recv_sem=a2a_recv.at[k, dz],
                device_id={"fgrp": target, "tile": tile, "pol": pol}, device_id_type=MESH,
            )
            turn.start()
            turns.append(turn)
    wide[z] = wide_send[z]
    thin[z] = thin_send[z]
    def partial(d, j):
        if j in thin_of:
            return thin[d, thin_of[j]].astype(jnp.float32)
        return wide[d, wide_of[j]]

    mine = block(u, v)
    half = depth // 2

    def landed(source):
        for k, ref in enumerate((wide, thin)):
            pltpu.make_async_remote_copy(
                src_ref=ref.at[source], dst_ref=ref.at[source], send_sem=a2a_send.at[k, 0],
                recv_sem=a2a_recv.at[k, (z - source + depth) % depth],
                device_id=partner, device_id_type=MESH,
            ).wait_recv()

    def finish(h):
        for source in range(h * half, (h + 1) * half):
            pl.when(z != source)(functools.partial(landed, source))
        for n in range(half):
            d = h * half + n
            for j in range(4):
                value = partial(d, j)
                if d > 0 and j < 3:
                    value = value + partial(d - 1, j + 4)
                own[h, :, 4 * n + j, :] = value
        out[mine, h] = own[h].astype(jnp.bfloat16)

    started = []
    columns, rows = [u, (u + 3) % 4, (u + 1) % 4, (u + 2) % 4], [v, (v + 3) % 4, (v + 1) % 4, (v + 2) % 4]

    def send(b, h, recv_sem, to):
        copy = pltpu.make_async_remote_copy(
            src_ref=out.at[b, h], dst_ref=out.at[b, h], send_sem=ag_send.at[len(started)],
            recv_sem=recv_sem, device_id=to, device_id_type=MESH,
        )
        copy.start()
        started.append(copy)

    def arrived(b, h, recv_sem):
        pltpu.make_async_remote_copy(
            src_ref=out.at[b, h], dst_ref=out.at[b, h], send_sem=ag_send.at[0],
            recv_sem=recv_sem, device_id=partner, device_id_type=MESH,
        ).wait_recv()

    def along_u(h):
        send(mine, h, ux_recv.at[h, 1], device(columns[2], v))
        send(mine, h, ux_recv.at[h, 2], device(columns[1], v))
        send(mine, h, ux_recv.at[h, 3], device(columns[3], v))
        send(mine, h, pt_recv.at[h, 0, 0], partner)

    def along_v(h, q):
        b = block(columns[q], v)
        if h == 0 or q == 0:
            send(b, h, vy_recv.at[h, q, 3], device(u, rows[3]))
        send(b, h, vy_recv.at[h, q, 1], device(u, rows[2]))
        send(b, h, vy_recv.at[h, q, 2], device(u, rows[1]))

    def across(h):
        send(mine, h, vy_recv.at[h, 3, 3], device(columns[3], rows[3]))
        send(mine, h, vy_recv.at[h, 3, 1], device(columns[3], rows[2]))
        send(mine, h, vy_recv.at[h, 3, 2], device(columns[3], rows[1]))
        send(mine, h, vy_recv.at[h, 1, 3], device(columns[2], rows[3]))
        send(mine, h, vy_recv.at[h, 2, 3], device(columns[1], rows[3]))

    def column(h, q):
        b = block(columns[q], v)
        arrived(b, h, ux_recv.at[h, q])
        if h == 0 or q < 3:
            along_v(h, q)
        send(b, h, pt_recv.at[h, q, 0], partner)

    def share(h, q):
        for r in (1, 2, 3):
            b = block(columns[q], rows[r])
            arrived(b, h, vy_recv.at[h, q, r])
            send(b, h, pt_recv.at[h, q, r], partner)

    finish(0)
    along_u(0)
    along_v(0, 0)
    finish(1)
    along_u(1)
    across(1)
    for q in (1, 2, 3):
        column(0, q)
    along_v(1, 0)
    share(0, 0)
    for q in (1, 2, 3):
        column(1, q)
    for q in (1, 2, 3):
        share(0, q)
    for q in range(4):
        share(1, q)
    for h in range(2):
        for q in range(4):
            for r in range(4):
                arrived(mine, h, pt_recv.at[h, q, r])
    for turn in turns:
        turn.wait_send()
    for copy in started:
        copy.wait_send()


def correlate_kernel(norm, blocks, out, vis, sems):
    mine = lax.axis_index("tile") * 2 + lax.axis_index("pol")
    count, channels = blocks.shape[0], blocks.shape[2]
    first = lax.broadcasted_iota(jnp.int32, (32, 128), 1) < 64

    def write(m, part):
        return pltpu.make_async_copy(vis.at[m, part], out.at[m, part], sems.at[m, part])

    def spectra(b, m):
        return jnp.concatenate([blocks[b, 0, m], blocks[b, 1, m]], axis=0)

    def channel(m, carry):
        a = spectra(mine, m)
        swapped = swap_halves(a)
        lhs = jnp.concatenate([a, jnp.where(first, swapped, -swapped)], axis=0)
        for q in range(0, count, 4):
            tiles = []
            for b in (q, q + 2):
                g, h = spectra(b, m), spectra(b + 1, m)
                re = jnp.where(first, g, swap_halves(h))
                im = jnp.where(first, swap_halves(g), h)
                tiles.append(jnp.concatenate([re, im], axis=0))
            rhs = jnp.concatenate(tiles, axis=1)
            product = lax.dot_general(
                lhs, rhs, (((0,), (0,)), ((), ())), preferred_element_type=jnp.float32
            ) * norm
            vis[m, 0, :, pl.ds(q * 64, 256)] = product[:64]
            vis[m, 1, :, pl.ds(q * 64, 256)] = product[64:]
        write(m, 0).start()
        write(m, 1).start()
        return carry

    lax.fori_loop(0, channels, channel, 0, unroll=True)
    for m in range(channels):
        write(m, 0).wait()
        write(m, 1).wait()


def body(voltages, gains):
    inputs, channels = voltages.shape[1], gains.shape[2]
    fgrp = lax.axis_size("fgrp")
    count = lax.axis_size("tile") * lax.axis_size("pol")
    spectra = voltages.shape[2] // NFFT * fgrp
    mine = channels // fgrp
    any_spec = pl.BlockSpec(memory_space=pltpu.HBM)
    vmem_spec = pl.BlockSpec(memory_space=pltpu.VMEM)
    dma = pltpu.SemaphoreType.DMA
    blocks = pl.pallas_call(
        spectra_kernel,
        out_shape=pltpu.VMEM((count, 2, mine, spectra // 2, 2 * inputs), jnp.bfloat16),
        in_specs=[any_spec] * 4,
        out_specs=vmem_spec,
        scratch_shapes=[
            pltpu.VMEM((4, 2, inputs, NFFT), jnp.bfloat16),
            pltpu.VMEM((2, inputs, channels), jnp.float32),
            pltpu.VMEM((TAPS, NFFT), jnp.float32),
            pltpu.VMEM((4, 8, NFFT), jnp.float32),
            pltpu.VMEM((12 * channels, NFFT), jnp.bfloat16),
            pltpu.VMEM((12 * channels, 8 * inputs), jnp.float32),
            pltpu.VMEM((fgrp, 4, mine, 2 * inputs), jnp.float32),
            pltpu.VMEM((fgrp, 4, mine, 2 * inputs), jnp.float32),
            pltpu.VMEM((fgrp, 3, mine, 2 * inputs), jnp.bfloat16),
            pltpu.VMEM((fgrp, 3, mine, 2 * inputs), jnp.bfloat16),
            pltpu.VMEM((2, mine, spectra // 2, 2 * inputs), jnp.float32),
            dma((7,)), dma((2, fgrp)), dma((2, fgrp)), dma((64,)), dma((2, 4)), dma((2, 4, 4)), dma((2, 4, 4)),
        ],
        compiler_params=pltpu.CompilerParams(
            collective_id=0, has_side_effects=True, vmem_limit_bytes=32 * 1024 * 1024
        ),
        name="spectra",
    )(*[
        pltpu.with_memory_space_constraint(operand, pltpu.HBM)
        for operand in (voltages, gains, jnp.asarray(tap_table()), jnp.asarray(rotation_table()))
    ])
    vis_shape = (mine, 2, inputs, count * inputs)
    return pl.pallas_call(
        functools.partial(correlate_kernel, 1.0 / math.sqrt(spectra)),
        out_shape=jax.ShapeDtypeStruct(vis_shape, jnp.float32),
        in_specs=[vmem_spec],
        out_specs=any_spec,
        scratch_shapes=[pltpu.VMEM(vis_shape, jnp.float32), dma((mine, 2))],
        compiler_params=pltpu.CompilerParams(vmem_limit_bytes=16 * 1024 * 1024),
        name="correlate",
    )(blocks)


def solution(mesh):
    return jax.shard_map(
        body,
        mesh=mesh,
        in_specs=(P(None, ("tile", "pol"), "fgrp"), P(None, ("tile", "pol"), None)),
        out_specs=P("fgrp", None, ("tile", "pol"), None),
        check_vma=False,
    )
```

```python
import functools
import math

import jax
import jax.numpy as jnp
import numpy as np
from jax import lax
from jax.experimental import pallas as pl
from jax.experimental.pallas import tpu as pltpu
from jax.sharding import PartitionSpec as P

NFFT = 4096
TAPS = 4
MESH = pl.DeviceIdType.MESH


def tap_table():
    total = TAPS * NFFT
    n = np.arange(total, dtype=np.float64)
    x = (n - total / 2 + 0.5) / NFFT
    window = 0.5 - 0.5 * np.cos(2.0 * np.pi * (n + 0.5) / total)
    taps = np.sinc(x) * window / math.sqrt(NFFT)
    return taps.reshape(TAPS, NFFT).astype(np.float32)


def rotation_table():
    k = np.arange(NFFT, dtype=np.int64)
    m = np.arange(8, dtype=np.int64)
    rows = []
    for step in (1, 8):
        angle = (k[None, :] * (step * m)[:, None] % NFFT) * (2.0 * np.pi / NFFT)
        rows += [np.cos(angle), np.sin(angle)]
    return np.stack(rows).astype(np.float32)


def swap_halves(v):
    return jnp.concatenate([v[:, 64:], v[:, :64]], axis=1)


def spectra_kernel(
    volt, gains, taps, rot, out,
    xbuf, gbuf, tbuf, rbuf, table, acc, wide_send, wide, thin_send, thin, own,
    in_sem, a2a_send, a2a_recv, ag_send, ux_recv, vy_recv, pt_recv,
):
    z, tile, pol = lax.axis_index("fgrp"), lax.axis_index("tile"), lax.axis_index("pol")
    depth = 8
    core, x, y = tile % 2, (tile // 2) % 4, pol * 2 + tile // 8
    u, v = x + core * (y - x), y + core * (x - y)

    def plane(u2, v2):
        x2, y2 = u2 + core * (v2 - u2), v2 + core * (u2 - v2)
        return ((y2 % 2) * 4 + x2) * 2 + core, y2 // 2

    def device(u2, v2):
        t2, p2 = plane(u2, v2)
        return {"fgrp": z, "tile": t2, "pol": p2}

    def block(u2, v2):
        t2, p2 = plane(u2, v2)
        return t2 * 2 + p2

    partner = {"fgrp": z, "tile": tile + 1 - 2 * core, "pol": pol}
    ring = [(z + dz) % depth for dz in range(depth)]

    barrier = pltpu.get_barrier_semaphore()
    plane_peers = [device((u + d) % 4, v) for d in (1, 2, 3)] + [device(u, (v + d) % 4) for d in (1, 2, 3)]
    plane_peers += [device((u + 2) % 4, (v + d) % 4) for d in (1, 2, 3)]
    plane_peers += [device((u + d) % 4, (v + 2) % 4) for d in (1, 3)]
    plane_peers.append(partner)
    for peer in plane_peers:
        pl.semaphore_signal(barrier, inc=1, device_id=peer, device_id_type=MESH)
    for dz in range(1, depth):
        pl.semaphore_signal(
            barrier, inc=1, device_id={"fgrp": ring[dz], "tile": tile, "pol": pol},
            device_id_type=MESH,
        )

    small = [
        pltpu.make_async_copy(rot, rbuf, in_sem.at[4]),
        pltpu.make_async_copy(taps, tbuf, in_sem.at[5]),
        pltpu.make_async_copy(gains, gbuf, in_sem.at[6]),
    ]
    frames = [
        pltpu.make_async_copy(volt.at[:, :, pl.ds(f * NFFT, NFFT)], xbuf.at[f], in_sem.at[f])
        for f in range(4)
    ]
    for copy in small + frames:
        copy.start()
    for copy in small:
        copy.wait()

    lanes = 256

    def make(i, carry):
        ks = pl.ds(pl.multiple_of(i * lanes, lanes), lanes)
        cb, sb = rbuf[0, :, ks], rbuf[1, :, ks]
        for a in range(0, 8, 2):
            cos, sin = [], []
            for step in (a, a + 1):
                ca, sa = rbuf[2, pl.ds(step, 1), ks], rbuf[3, pl.ds(step, 1), ks]
                cos.append(cb * ca - sb * sa)
                sin.append(sb * ca + cb * sa)
            for first, rows in ((0, cos), (64, sin)):
                value = jnp.concatenate(rows, axis=0)
                row = first + a * 8
                for t in (1, 2):
                    tapped = value * tbuf[pl.ds(t, 1), ks]
                    rounded = tapped.astype(jnp.bfloat16)
                    low = tapped - rounded.astype(jnp.float32)
                    table[pl.ds((t - 1) * 256 + row, 16), ks] = rounded
                    table[pl.ds((t - 1) * 256 + 128 + row, 16), ks] = low.astype(jnp.bfloat16)
                for t, base in ((0, 512), (3, 640)):
                    tapped = value * tbuf[pl.ds(t, 1), ks]
                    table[pl.ds(base + row, 16), ks] = tapped.astype(jnp.bfloat16)
        return carry

    lax.fori_loop(0, NFFT // lanes, make, 0)
    lane = lax.broadcasted_iota(jnp.int32, (64, 128), 1)
    sign = jnp.where(lane < 64, 1.0, -1.0).astype(jnp.float32)
    g_re = jnp.transpose(jnp.concatenate([gbuf[0], gbuf[0]], axis=0))
    g_im = jnp.transpose(jnp.concatenate([gbuf[1], gbuf[1]], axis=0)) * -sign
    for copy in frames:
        copy.wait()
    acc[...] = lax.dot_general(
        table[...], xbuf[...].reshape(acc.shape[1], NFFT), (((1,), (1,)), ((), ())),
        preferred_element_type=jnp.float32,
    )

    thin_of, wide_of = {0: 0, 3: 1, 6: 2}, {1: 0, 2: 1, 4: 2, 5: 3}
    for j in range(7):
        total = None
        for f in range(4):
            t = f - j + 3
            if 0 <= t < TAPS:
                fs = pl.ds(f * 128, 128)
                base = (512, 0, 256, 640)[t]
                term = acc[pl.ds(base, 128), fs]
                if t in (1, 2):
                    term = term + acc[pl.ds(base + 128, 128), fs]
                total = term if total is None else total + term
        raw = total[:64] + sign * swap_halves(total[64:])
        gained = g_re * raw + g_im * swap_halves(raw)
        for c in range(depth):
            if j in thin_of:
                thin_send[c, thin_of[j]] = gained[8 * c : 8 * c + 8].astype(jnp.bfloat16)
            else:
                wide_send[c, wide_of[j]] = gained[8 * c : 8 * c + 8]

    pl.semaphore_wait(barrier, depth + 11)
    turns = []
    for n in range(depth - 1):
        target = n + jnp.where(z <= n, 1, 0)
        dz = (target - z + depth) % depth
        for k, (ours, theirs) in enumerate(((wide_send, wide), (thin_send, thin))):
            turn = pltpu.make_async_remote_copy(
                src_ref=ours.at[target], dst_ref=theirs.at[z],
                send_sem=a2a_send.at[k, dz], recv_sem=a2a_recv.at[k, dz],
                device_id={"fgrp": target, "tile": tile, "pol": pol}, device_id_type=MESH,
            )
            turn.start()
            turns.append(turn)
    wide[z] = wide_send[z]
    thin[z] = thin_send[z]
    def partial(d, j):
        if j in thin_of:
            return thin[d, thin_of[j]].astype(jnp.float32)
        return wide[d, wide_of[j]]

    mine = block(u, v)
    half = depth // 2

    def landed(source):
        for k, ref in enumerate((wide, thin)):
            pltpu.make_async_remote_copy(
                src_ref=ref.at[source], dst_ref=ref.at[source], send_sem=a2a_send.at[k, 0],
                recv_sem=a2a_recv.at[k, (z - source + depth) % depth],
                device_id=partner, device_id_type=MESH,
            ).wait_recv()

    def finish(h):
        for source in range(h * half, (h + 1) * half):
            pl.when(z != source)(functools.partial(landed, source))
        for n in range(half):
            d = h * half + n
            for j in range(4):
                value = partial(d, j)
                if d > 0 and j < 3:
                    value = value + partial(d - 1, j + 4)
                own[h, :, 4 * n + j, :] = value
        out[mine, h] = own[h].astype(jnp.bfloat16)

    started = []
    columns, rows = [u, (u + 3) % 4, (u + 1) % 4, (u + 2) % 4], [v, (v + 3) % 4, (v + 1) % 4, (v + 2) % 4]

    def send(b, h, recv_sem, to):
        copy = pltpu.make_async_remote_copy(
            src_ref=out.at[b, h], dst_ref=out.at[b, h], send_sem=ag_send.at[len(started)],
            recv_sem=recv_sem, device_id=to, device_id_type=MESH,
        )
        copy.start()
        started.append(copy)

    def arrived(b, h, recv_sem):
        pltpu.make_async_remote_copy(
            src_ref=out.at[b, h], dst_ref=out.at[b, h], send_sem=ag_send.at[0],
            recv_sem=recv_sem, device_id=partner, device_id_type=MESH,
        ).wait_recv()

    def along_u(h):
        send(mine, h, ux_recv.at[h, 1], device(columns[2], v))
        send(mine, h, ux_recv.at[h, 2], device(columns[1], v))
        send(mine, h, ux_recv.at[h, 3], device(columns[3], v))
        send(mine, h, pt_recv.at[h, 0, 0], partner)

    def along_v(h, q):
        b = block(columns[q], v)
        if h == 0 or q == 0:
            send(b, h, vy_recv.at[h, q, 3], device(u, rows[3]))
        send(b, h, vy_recv.at[h, q, 1], device(u, rows[2]))
        send(b, h, vy_recv.at[h, q, 2], device(u, rows[1]))

    def across(h):
        send(mine, h, vy_recv.at[h, 3, 3], device(columns[3], rows[3]))
        send(mine, h, vy_recv.at[h, 3, 1], device(columns[3], rows[2]))
        send(mine, h, vy_recv.at[h, 3, 2], device(columns[3], rows[1]))
        send(mine, h, vy_recv.at[h, 1, 3], device(columns[2], rows[3]))
        send(mine, h, vy_recv.at[h, 2, 3], device(columns[1], rows[3]))

    def column(h, q):
        b = block(columns[q], v)
        arrived(b, h, ux_recv.at[h, q])
        if h == 0 or q < 3:
            along_v(h, q)
        send(b, h, pt_recv.at[h, q, 0], partner)

    def share(h, q, offsets=(1, 2, 3)):
        for r in offsets:
            b = block(columns[q], rows[r])
            arrived(b, h, vy_recv.at[h, q, r])
            send(b, h, pt_recv.at[h, q, r], partner)

    finish(0)
    along_u(0)
    along_v(0, 0)
    finish(1)
    along_u(1)
    across(1)
    for q in (1, 2, 3):
        column(0, q)
    along_v(1, 0)
    share(0, 0)
    for q in (1, 2, 3):
        column(1, q)
    for q in (1, 2, 3):
        share(0, q)
    share(1, 0)
    share(1, 3)
    for q in (1, 2):
        share(1, q, (3,))
    for q in (1, 2):
        share(1, q, (1, 2))
    for h in range(2):
        for q in range(4):
            for r in range(4):
                arrived(mine, h, pt_recv.at[h, q, r])
    for turn in turns:
        turn.wait_send()
    for copy in started:
        copy.wait_send()


def correlate_kernel(norm, blocks, out, vis, sems):
    mine = lax.axis_index("tile") * 2 + lax.axis_index("pol")
    count, channels = blocks.shape[0], blocks.shape[2]
    first = lax.broadcasted_iota(jnp.int32, (32, 128), 1) < 64

    def write(m, part):
        return pltpu.make_async_copy(vis.at[m, part], out.at[m, part], sems.at[m, part])

    def spectra(b, m):
        return jnp.concatenate([blocks[b, 0, m], blocks[b, 1, m]], axis=0)

    def channel(m, carry):
        a = spectra(mine, m)
        swapped = swap_halves(a)
        lhs = jnp.concatenate([a, jnp.where(first, swapped, -swapped)], axis=0)
        for q in range(0, count, 4):
            tiles = []
            for b in (q, q + 2):
                g, h = spectra(b, m), spectra(b + 1, m)
                re = jnp.where(first, g, swap_halves(h))
                im = jnp.where(first, swap_halves(g), h)
                tiles.append(jnp.concatenate([re, im], axis=0))
            rhs = jnp.concatenate(tiles, axis=1)
            product = lax.dot_general(
                lhs, rhs, (((0,), (0,)), ((), ())), preferred_element_type=jnp.float32
            ) * norm
            vis[m, 0, :, pl.ds(q * 64, 256)] = product[:64]
            vis[m, 1, :, pl.ds(q * 64, 256)] = product[64:]
        write(m, 0).start()
        write(m, 1).start()
        return carry

    lax.fori_loop(0, channels, channel, 0, unroll=True)
    for m in range(channels):
        write(m, 0).wait()
        write(m, 1).wait()


def body(voltages, gains):
    inputs, channels = voltages.shape[1], gains.shape[2]
    fgrp = lax.axis_size("fgrp")
    count = lax.axis_size("tile") * lax.axis_size("pol")
    spectra = voltages.shape[2] // NFFT * fgrp
    mine = channels // fgrp
    any_spec = pl.BlockSpec(memory_space=pltpu.HBM)
    vmem_spec = pl.BlockSpec(memory_space=pltpu.VMEM)
    dma = pltpu.SemaphoreType.DMA
    blocks = pl.pallas_call(
        spectra_kernel,
        out_shape=pltpu.VMEM((count, 2, mine, spectra // 2, 2 * inputs), jnp.bfloat16),
        in_specs=[any_spec] * 4,
        out_specs=vmem_spec,
        scratch_shapes=[
            pltpu.VMEM((4, 2, inputs, NFFT), jnp.bfloat16),
            pltpu.VMEM((2, inputs, channels), jnp.float32),
            pltpu.VMEM((TAPS, NFFT), jnp.float32),
            pltpu.VMEM((4, 8, NFFT), jnp.float32),
            pltpu.VMEM((12 * channels, NFFT), jnp.bfloat16),
            pltpu.VMEM((12 * channels, 8 * inputs), jnp.float32),
            pltpu.VMEM((fgrp, 4, mine, 2 * inputs), jnp.float32),
            pltpu.VMEM((fgrp, 4, mine, 2 * inputs), jnp.float32),
            pltpu.VMEM((fgrp, 3, mine, 2 * inputs), jnp.bfloat16),
            pltpu.VMEM((fgrp, 3, mine, 2 * inputs), jnp.bfloat16),
            pltpu.VMEM((2, mine, spectra // 2, 2 * inputs), jnp.float32),
            dma((7,)), dma((2, fgrp)), dma((2, fgrp)), dma((64,)), dma((2, 4)), dma((2, 4, 4)), dma((2, 4, 4)),
        ],
        compiler_params=pltpu.CompilerParams(
            collective_id=0, has_side_effects=True, vmem_limit_bytes=32 * 1024 * 1024
        ),
        name="spectra",
    )(*[
        pltpu.with_memory_space_constraint(operand, pltpu.HBM)
        for operand in (voltages, gains, jnp.asarray(tap_table()), jnp.asarray(rotation_table()))
    ])
    vis_shape = (mine, 2, inputs, count * inputs)
    return pl.pallas_call(
        functools.partial(correlate_kernel, 1.0 / math.sqrt(spectra)),
        out_shape=jax.ShapeDtypeStruct(vis_shape, jnp.float32),
        in_specs=[vmem_spec],
        out_specs=any_spec,
        scratch_shapes=[pltpu.VMEM(vis_shape, jnp.float32), dma((mine, 2))],
        compiler_params=pltpu.CompilerParams(vmem_limit_bytes=16 * 1024 * 1024),
        name="correlate",
    )(blocks)


def solution(mesh):
    return jax.shard_map(
        body,
        mesh=mesh,
        in_specs=(P(None, ("tile", "pol"), "fgrp"), P(None, ("tile", "pol"), None)),
        out_specs=P("fgrp", None, ("tile", "pol"), None),
        check_vma=False,
    )
```
